512 devices in a mesh: ha: 8 (over y_lo, core), az: 64 (over x, z, y_hi).
Axes of the slice: x: 4, y: 8 (y_hi: 2, y_lo: 4; y = y_hi * 4 + y_lo), z: 8, core: 2. Of those that a mesh axis runs over, the one named last changes fastest.
Arguments:
- field: float32 [2, 4096, 8192], P(None, 'ha', 'az'), may hold values from -6 to 6
- terrain: int32 [8192], P('az'), may hold values from 0 to 63
- profile_pick: int32 [8192], P('az'), may hold values from 0 to 15
- profile_table: float32 [16, 4096], replicated, may hold values from -3.140625 to 3.140625
- clutter_mask: int32 [128, 8192], P(None, 'az'), may hold values 0 or 1
- pulse: float32 [63], replicated, may hold values from -0.6 to 0.6
- beam: float32 [31], replicated, may hold values from -0.9 to 0.9
- measured: float32 [2, 128, 8192], P(None, None, 'az'), may hold values from -6 to 6
Outputs:
- field_out: float32 [2, 4096, 8192], P(None, 'ha', 'az')
- sources: float32 [2, 2, 128, 8192], P(None, None, 'ha', 'az')
The draws below stay inside these ranges and needn't reach their ends.
All inputs are finite; a program needn't handle non-finite values. No bound on the sum of `clutter_mask` on one device may be relied on, other than what follows from the above.
Results may differ from the reference program's by a relative error of at most 0.00022.
Values sent between devices are 32-bit elements; how exact they have to be, the bound alone decides.
No kernel may reach another device: no remote copies, remote signals or barrier semaphores. Data moves between devices by JAX's collectives and lax.ppermute only.
A program may use at most 64 MiB of HBM per device.

```python
import math
import jax
import jax.numpy as jnp
from jax import lax

NH = 4096
NA = 8192
BOT = 128
RTAPS = 63
ATAPS = 31
NPROF = 16
STEPS = 2


def plant(values, own_key, low, largest):
    spot = [jax.random.randint(jax.random.fold_in(own_key, axis), (), 0, length) for axis, length in enumerate(values.shape)]
    widest = values.shape.index(max(values.shape))
    beside = spot[:widest] + [(spot[widest] + 1) % values.shape[widest]] + spot[widest + 1:]
    return values.at[tuple(spot)].set(low).at[tuple(beside)].set(largest)


def shard_levels(stream_key, shape, pieces, low, high):
    level = 1.0
    for position, blocks in pieces:
        steps = jax.random.uniform(jax.random.fold_in(jax.random.fold_in(stream_key, 6), position), (blocks,), jnp.float32, low / len(pieces), high / len(pieces))
        level = level * jnp.repeat(jnp.exp(steps), shape[position] // blocks).reshape((-1,) + (1,) * (len(shape) - 1 - position))
    return level


def normal_values(key, shape, width, limit, cuts=(), held_as=jnp.bfloat16):
    values = width * jax.random.normal(key, shape, jnp.float32)
    if cuts:
        values = values * shard_levels(key, shape, cuts, -0.22, 0.18)
    return jnp.clip(values, -limit, limit).astype(held_as)


def setup_inputs(seed: int = 0) -> dict:
    streams_of = jax.random.split(jax.random.key(seed), 9)
    return {
        "field": normal_values(streams_of[0], (2, NH, NA), 1.0, 6.0, ((1, 8), (2, 64)), jnp.float32),
        "terrain": plant(jax.random.randint(streams_of[1], (NA,), 0, BOT // 2), jax.random.fold_in(streams_of[1], 1), 0, (BOT // 2) - 1).astype(jnp.int32),
        "profile_pick": plant(jax.random.randint(streams_of[2], (NA,), 0, NPROF), jax.random.fold_in(streams_of[2], 1), 0, NPROF - 1).astype(jnp.int32),
        "profile_table": jnp.clip(jax.random.uniform(streams_of[3], (NPROF, NH), jnp.float32, -3.140625, 3.140625), -3.140625, 3.140625),
        "clutter_mask": plant((jax.random.randint(streams_of[4], (BOT, NA), 0, 4) < 3).astype(jnp.int32), jax.random.fold_in(streams_of[4], 1), 0, 1),
        "pulse": normal_values(streams_of[5], (RTAPS,), 0.126, 0.6, (), jnp.float32),
        "beam": normal_values(streams_of[6], (ATAPS,), 0.18, 0.9, (), jnp.float32),
        "measured": normal_values(streams_of[7], (STEPS, BOT, NA), 1.0, 6.0, ((2, 64),), jnp.float32),
    }


height_chirp = 1
azimuth_chirp = 3


def chirp_angle(count, spread):
    index = jnp.arange(count, dtype=jnp.int32)
    return ((spread * index * index) % (2 * count)).astype(jnp.float32) * (-math.pi / count)


def screen_coef(rows, terr, phase, total):
    height = rows.astype(jnp.float32)
    depth = jnp.maximum(height - 0.75 * total, 0.0) / (0.25 * total)
    amount = jnp.exp(-4.0 * depth * depth) * (rows >= terr).astype(jnp.float32)
    return amount * jnp.cos(phase), amount * jnp.sin(phase)


def range_band(pulse, bottom):
    taps = pulse.shape[0]
    half = (taps - 1) // 2
    row = lax.broadcasted_iota(jnp.int32, (bottom, bottom), 0)
    col = lax.broadcasted_iota(jnp.int32, (bottom, bottom), 1)
    offset = col - row + half
    hit = offset[:, :, None] == jnp.arange(taps, dtype=jnp.int32)[None, None, :]
    return jnp.sum(jnp.where(hit, pulse[None, None, :], 0.0), axis=-1)


def reference(field, terrain, profile_pick, profile_table, clutter_mask, pulse, beam, measured):
    highest = lax.Precision.HIGHEST
    rows = jnp.arange(NH, dtype=jnp.int32)[:, None]
    phase = jnp.take(profile_table, profile_pick, axis=0).T
    coef_re, coef_im = screen_coef(rows, terrain[None, :], phase, NH)
    coef = coef_re + 1j * coef_im
    angle_z = chirp_angle(NH, height_chirp)
    angle_y = chirp_angle(NA, azimuth_chirp)
    kern_z = jnp.cos(angle_z) + 1j * jnp.sin(angle_z)
    kern_y = jnp.cos(angle_y) + 1j * jnp.sin(angle_y)
    mask = clutter_mask.astype(jnp.float32)
    rmat = range_band(pulse, BOT)
    half_beam = (ATAPS - 1) // 2
    wave = field[0] + 1j * field[1]
    result = []
    for step in range(STEPS):
        wave = jnp.fft.ifft(jnp.fft.fft(wave, axis=1) * kern_y[None, :], axis=1)
        wave = jnp.fft.ifft(jnp.fft.fft(wave, axis=0) * kern_z[:, None], axis=0)
        wave = wave * coef
        low_re = jnp.real(wave[:BOT])
        low_im = jnp.imag(wave[:BOT])
        power = mask * (low_re * low_re + low_im * low_im)
        ranged = jnp.dot(rmat, power, precision=highest)
        model = jnp.zeros_like(ranged)
        for tap in range(ATAPS):
            model = model + beam[tap] * jnp.roll(ranged, half_beam - tap, axis=1)
        misfit = model - measured[step]
        spread_back = jnp.zeros_like(misfit)
        for tap in range(ATAPS):
            spread_back = spread_back + beam[tap] * jnp.roll(misfit, tap - half_beam, axis=1)
        back = jnp.dot(rmat.T, spread_back, precision=highest)
        result.append(jnp.stack([2.0 * mask * low_re * back, 2.0 * mask * low_im * back]))
    field_out = jnp.stack([jnp.real(wave), jnp.imag(wave)])
    return field_out, jnp.stack(result)
```

```python
import functools
import math

import jax
import jax.numpy as jnp
import numpy as np
from jax import lax
from jax.experimental import pallas as pl
from jax.experimental.pallas import tpu as pltpu
from jax.sharding import PartitionSpec as P

NH, NA = 4096, 8192
PH, PA = 8, 64
ROWS = PH * PA
LANES = 128
BOT = 128
height_chirp = 1
azimuth_chirp = 3
INV = pow(azimuth_chirp, -1, 2 * NA)
HIGHEST = lax.Precision.HIGHEST


def gauss(count, spread):
    index = np.arange(count, dtype=np.int64)
    return np.sum(np.exp(-1j * np.pi * ((spread * index * index) % (2 * count)) / count)) / count


GAIN = gauss(NH, height_chirp) * gauss(NA, azimuth_chirp)


def row_matrices():
    turn = 2.0 * np.pi * ((INV * np.outer(np.arange(PA), np.arange(PA))) % PA) / PA
    re, im = np.cos(turn), -np.sin(turn)
    split = np.block([[re, -im], [im, re]])
    mixed = split.reshape(2 * PA, 2, PA).transpose(0, 2, 1).reshape(2 * PA, 2 * PA)
    return split.astype(np.float32), mixed.astype(np.float32)


SPLIT_DFT, MIXED_DFT = row_matrices()


def pair_choice():
    table = np.zeros((4, LANES, LANES), np.float32)
    for part in range(4):
        for q in range(2):
            for o in range(8):
                for j in range(2):
                    table[part, 64 * q + 2 * o + j, 16 * o + 2 * (2 * part + q) + j] = 1.0
    return table.reshape(4 * LANES, LANES)


PAIRS = pair_choice()


def dot(left, right):
    return jnp.dot(left, right, precision=HIGHEST, preferred_element_type=jnp.float32)


def lane_of(shape):
    return lax.broadcasted_iota(jnp.int32, shape, len(shape) - 1)


def row_of(shape):
    return lax.broadcasted_iota(jnp.int32, shape, len(shape) - 2)


def dft4(re, im):
    sr, si = re[0] + re[2], im[0] + im[2]
    dr, di = re[0] - re[2], im[0] - im[2]
    tr, ti = re[1] + re[3], im[1] + im[3]
    ur, ui = re[1] - re[3], im[1] - im[3]
    return [sr + tr, dr + ui, sr - tr, dr - ui], [si + ti, di - ur, si - ti, di + ur]


def dft8(re, im):
    half = math.sqrt(0.5)
    er, ei = dft4(re[0::2], im[0::2])
    pr, pi = dft4(re[1::2], im[1::2])
    tr = [pr[0], half * (pr[1] + pi[1]), pi[2], half * (pi[3] - pr[3])]
    ti = [pi[0], half * (pi[1] - pr[1]), -pr[2], -half * (pr[3] + pi[3])]
    out_re = [er[k] + tr[k] for k in range(4)] + [er[k] - tr[k] for k in range(4)]
    out_im = [ei[k] + ti[k] for k in range(4)] + [ei[k] - ti[k] for k in range(4)]
    return out_re, out_im


def dft8_group(held, group):
    low = 8 * group
    re = [held[i * 128 + low : i * 128 + low + 8, :] for i in range(8)]
    im = [held[i * 128 + 64 + low : i * 128 + 64 + low + 8, :] for i in range(8)]
    return dft8(re, im)


def flip_halves(block):
    turned = jnp.concatenate([block, block], axis=0).T
    return jnp.where(lane_of((64, LANES)) < 64, turned[:64], turned[64:])


def pack_kernel(place, field, terrain, pick, mask, turned, out):
    dh, da = place[0], place[1]
    lanes = lane_of((64, LANES))
    rows = row_of((64, LANES))
    pads = [
        terrain[...].astype(jnp.float32),
        pick[...].astype(jnp.float32),
        jnp.zeros((14, LANES), jnp.float32),
        mask[pl.ds(pl.multiple_of(16 * dh, 16), 16), :].astype(jnp.float32),
    ]
    stacked = jnp.concatenate([jnp.zeros((64, LANES), jnp.float32)] + pads + pads, axis=0)
    upright = stacked.T
    common = jnp.where(lanes < 96, upright[:64], upright[64:])
    lane8 = lane_of((8, LANES))
    head = jnp.zeros((8, LANES), jnp.float32)
    tail = jnp.zeros((8, LANES), jnp.float32)
    for s in range(2):
        for j in range(2):
            slot = 2 * s + j
            part = turned.at[s][pl.ds(dh + 8 * j, 8, stride=16), :]
            here = (lane8 >= 16 * slot) & (lane8 < 16 * slot + 16)
            first = part if slot == 0 else pltpu.roll(part, 16 * slot, 1)
            head = jnp.where(here, first, head)
            tail = jnp.where(here, pltpu.roll(part, 16 + 16 * slot, 1), tail)
    right = lax.rem(da + 1, PA)
    left = lax.rem(da + PA - 1, PA)
    for e in range(8):
        spread_tail = jnp.broadcast_to(tail[e : e + 1, :], (64, LANES))
        spread_head = jnp.broadcast_to(head[e : e + 1, :], (64, LANES))
        edge = jnp.where(rows == right, spread_tail, jnp.where(rows == left, spread_head, 0.0))
        for c in range(2):
            out[pl.ds(e * 192 + c, 64, stride=3), :] = flip_halves(
                field.at[c][pl.ds(e, 64, stride=8), :]
            )
        out[pl.ds(e * 192 + 2, 64, stride=3), :] = jnp.where(lanes < 64, edge, common)


def finish_send(held, twist_re, twist_im, lane_dft, out, mid_re, mid_im):
    for group in range(8):
        re, im = dft8_group(held, group)
        for k in range(8):
            at = slice(k * 64 + 8 * group, k * 64 + 8 * group + 8)
            tr, ti = twist_re[at, :], twist_im[at, :]
            mid_re[at, :] = re[k] * tr - im[k] * ti
            mid_im[at, :] = re[k] * ti + im[k] * tr
    from_re = dot(mid_re[...], lane_dft[...])
    from_im = dot(mid_im[...], lane_dft[...])
    out[pl.ds(0, ROWS, stride=2), :] = from_re[:, :LANES] - from_im[:, LANES:]
    out[pl.ds(1, ROWS, stride=2), :] = from_re[:, LANES:] + from_im[:, :LANES]


def first_kernel(got, chirp_re, chirp_im, twist_re, twist_im, lane_dft, split, out, held, mid_re, mid_im):
    for i in range(8):
        xr = got[pl.ds(i * 192, 64, stride=3), :]
        xi = got[pl.ds(i * 192 + 1, 64, stride=3), :]
        at = slice(i * 64, i * 64 + 64)
        dr, di = chirp_re[at, :], chirp_im[at, :]
        both = jnp.concatenate([xr * dr - xi * di, xr * di + xi * dr], axis=0)
        held[i * 128 : (i + 1) * 128, :] = dot(split[...], both)
    finish_send(held, twist_re, twist_im, lane_dft, out, mid_re, mid_im)


def middle_kernel(
    got, coef_re, coef_im, both_re, both_im, twist_re, twist_im, lane_dft, split, mixed,
    out, strip, held, mid_re, mid_im, next_in,
):
    for i in range(8):
        held[i * 128 : (i + 1) * 128, :] = dot(mixed[...], got[i * 128 : (i + 1) * 128, :])
    for group in range(8):
        re, im = dft8_group(held, group)
        low = 8 * group
        cr, ci = coef_re[low : low + 8, :], coef_im[low : low + 8, :]
        strip[0, low : low + 8, :] = re[0] * cr - im[0] * ci
        strip[1, low : low + 8, :] = re[0] * ci + im[0] * cr
        for k in range(8):
            at = slice(k * 64 + low, k * 64 + low + 8)
            cr, ci = both_re[at, :], both_im[at, :]
            next_in[k * 128 + low : k * 128 + low + 8, :] = re[k] * cr - im[k] * ci
            next_in[k * 128 + 64 + low : k * 128 + 64 + low + 8, :] = re[k] * ci + im[k] * cr
    for i in range(8):
        held[i * 128 : (i + 1) * 128, :] = dot(split[...], next_in[i * 128 : (i + 1) * 128, :])
    finish_send(held, twist_re, twist_im, lane_dft, out, mid_re, mid_im)


def last_kernel(place, got, coef_re, coef_im, strip, seen, pairs, mixed, out, held, low_re, low_im):
    f = place[1]
    for i in range(8):
        held[i * 128 : (i + 1) * 128, :] = dot(mixed[...], got[i * 128 : (i + 1) * 128, :])
    for group in range(8):
        re, im = dft8_group(held, group)
        low = 8 * group
        for k in range(8):
            at = slice(k * 64 + low, k * 64 + low + 8)
            cr, ci = coef_re[at, :], coef_im[at, :]
            new_re = re[k] * cr - im[k] * ci
            new_im = re[k] * ci + im[k] * cr
            out[pl.ds(3 * (k * 64 + low), 8, stride=3), :] = new_re
            out[pl.ds(3 * (k * 64 + low) + 1, 8, stride=3), :] = new_im
            if k == 0:
                low_re[low : low + 8, :] = new_re
                low_im[low : low + 8, :] = new_im
    lanes = lane_of((64, LANES))
    parts = [strip[0], strip[1], low_re[...], low_im[...]]
    chosen = dot(parts[0], pairs[0:LANES, :])
    for part in range(1, 4):
        chosen = chosen + dot(parts[part], pairs[part * LANES : (part + 1) * LANES, :])
    powers = jnp.zeros((64, LANES), jnp.float32)
    for s in range(2):
        power = seen[...] * (parts[2 * s] * parts[2 * s] + parts[2 * s + 1] * parts[2 * s + 1])
        base = 48 * s
        after = pltpu.roll(power, PA - 1, 0)
        before = pltpu.roll(power, 1, 0)
        near = power if base == 0 else pltpu.roll(power, base, 1)
        other = pltpu.roll(power, base + 16 + 64, 1)
        side = jnp.where(
            f < 32, pltpu.roll(after, base + 32, 1), pltpu.roll(before, (base + 32 + 64) % LANES, 1)
        )
        for slot, moved in enumerate((near, other, side)):
            at = base + 16 * slot
            powers = jnp.where((lanes >= at) & (lanes < at + 16), moved, powers)
    for o in range(8):
        shift = (96 - 16 * o) % LANES
        moved = chosen if shift == 0 else pltpu.roll(chosen, shift, 1)
        out[pl.ds(o * 192 + 2, 64, stride=3), :] = jnp.where(lanes < 96, powers, moved)


def unpack_kernel(place, got, mask, back_measured, range_pair, beam_pair, field_out, sources, turned):
    eh = place[0]
    for e in range(8):
        for c in range(2):
            field_out.at[c][pl.ds(e, 64, stride=8), :] = flip_halves(
                got[pl.ds(e * 192 + c, 64, stride=3), :]
            )
        aux = got[pl.ds(e * 192 + 2, 64, stride=3), :]
        turned[e * 128 : (e + 1) * 128, :] = jnp.concatenate([aux, aux], axis=0).T
    seen = mask[pl.ds(pl.multiple_of(16 * eh, 16), 16), :].astype(jnp.float32)
    lane8 = lane_of((8, LANES))
    for s in range(2):
        back = -back_measured[s]
        for slot in range(3):
            at = 48 * s + 16 * slot
            gathered = jnp.concatenate(
                [turned[e * 128 + at : e * 128 + at + 16, :] for e in range(8)], axis=0
            )
            ranged = dot(range_pair[...], gathered)
            back = back + dot(ranged, beam_pair[slot])
        for c in range(2):
            for j in range(2):
                at = 96 + 2 * (4 * s + 2 * c) + j
                near = turned[pl.ds(at, 8, stride=128), :]
                far = turned[pl.ds(at + 2, 8, stride=128), :]
                value = jnp.where(lane8 < 64, near, far)
                sources[s, c, 8 * j : 8 * j + 8, :] = (
                    2.0 * seen[8 * j : 8 * j + 8] * value * back[8 * j : 8 * j + 8]
                )


def prepare_kernel(
    place, got, profile, turned, beam_mix, chirp_re, chirp_im,
    coef_re, coef_im, both_re, both_im, seen, back_measured, edge,
):
    e, f = place[0], place[1]
    lanes = lane_of((64, LANES))
    rows = row_of((64, LANES))
    square = lane_of((LANES, LANES))
    down = row_of((LANES, LANES))
    total = jnp.zeros((64, LANES), jnp.float32)
    left = lax.rem(f + PA - 1, PA)
    right = lax.rem(f + 1, PA)
    first = got[pl.ds(2, 64, stride=3), :]
    for dh in range(8):
        aux = first if dh == 0 else got[pl.ds(dh * 192 + 2, 64, stride=3), :]
        j = lax.rem(square, 64) - 2 * dh
        wanted = 80 + 32 * (square // 64) + 8 * j + e
        choose = jnp.where((j >= 0) & (j < 2) & (down == wanted), 1.0, 0.0)
        total = total + jnp.dot(aux, choose, preferred_element_type=jnp.float32)
        edge[dh : dh + 1, :] = jnp.sum(jnp.where(rows == left, aux, 0.0), axis=0, keepdims=True)
        edge[8 + dh : 9 + dh, :] = jnp.sum(jnp.where(rows == right, aux, 0.0), axis=0, keepdims=True)
    seen[...] = total
    for s in range(2):
        for j in range(2):
            slot = 2 * s + j
            start = pl.multiple_of(16 * e + 8 * j, 8)
            own = dot(turned.at[s][pl.ds(start, 8), :], beam_mix[LANES : 2 * LANES, :])
            shift = (LANES - 16 * slot) % LANES
            near = edge[0:8, :] if shift == 0 else pltpu.roll(edge[0:8, :], shift, 1)
            far = edge[8:16, :] if shift == 0 else pltpu.roll(edge[8:16, :], shift, 1)
            own = own + dot(near, beam_mix[0:LANES, :])
            own = own + dot(far, beam_mix[2 * LANES : 3 * LANES, :])
            back_measured[s, 8 * j : 8 * j + 8, :] = own

    def column(lane):
        return jnp.sum(jnp.where(lanes == lane, first, 0.0), axis=1, keepdims=True)

    pick0, pick1 = column(65), column(97)
    onehot = jnp.where(lanes < 16, pick0, pick1 + 16.0) == lanes.astype(jnp.float32)
    onehot = jnp.where(onehot & (lanes < 32), 1.0, 0.0)
    ground = jnp.where(lanes < 64, column(64), column(96))
    tall = row_of((512, LANES))
    choose = jnp.where(tall == 8 * lax.rem(lane_of((512, LANES)), 64) + e, 1.0, 0.0)
    lane16 = lane_of((16, LANES))
    for i in range(8):
        phase = dot(profile[:, 512 * i : 512 * (i + 1)], choose)
        height = 512 * i + 8 * lax.rem(lane16, 64) + e
        depth = jnp.maximum(height.astype(jnp.float32) - 0.75 * NH, 0.0) / (0.25 * NH)
        amount = abs(GAIN) * jnp.exp(-4.0 * depth * depth)
        angle = phase + float(np.angle(GAIN))
        pair = []
        for value in (amount * jnp.cos(angle), amount * jnp.sin(angle)):
            lower = jnp.where(lane16 < 64, value, 0.0)
            upper = jnp.where(lane16 < 64, 0.0, value)
            pair.append(
                dot(onehot, jnp.concatenate([lower, upper, jnp.zeros((96, LANES), jnp.float32)], axis=0))
            )
        at = slice(i * 64, i * 64 + 64)
        above = (512 * i + 8 * lax.rem(lanes, 64) + e).astype(jnp.float32) >= ground
        sr = jnp.where(above, pair[0], 0.0)
        si = jnp.where(above, pair[1], 0.0)
        dr, di = chirp_re[at, :], chirp_im[at, :]
        cr, ci = sr * dr - si * di, sr * di + si * dr
        coef_re[at, :] = cr
        coef_im[at, :] = ci
        both_re[at, :] = cr * dr - ci * di
        both_im[at, :] = cr * di + ci * dr


def turns(steps, modulus):
    angle = (steps % modulus).astype(jnp.float32) * (2.0 * math.pi / modulus)
    return jnp.cos(angle), jnp.sin(angle)


def layout_tables(e, f):
    row = lax.broadcasted_iota(jnp.int32, (ROWS, LANES), 0)
    lane = lax.broadcasted_iota(jnp.int32, (ROWS, LANES), 1)
    i, b = row // PA, row % PA
    q, r = lane // 64, lane % 64
    square_h = 64 * r * r + e * e + 1024 * i * e + 16 * r * e
    square_a = INV * (4096 * q * q + f * f + 128 * q * f) + ((256 * INV) % (2 * NA)) * b * f
    chirp = turns(2 * square_h + square_a, 2 * NA)
    twist = turns(-(16 * i * r + ((64 * INV) % NA) * b * q + 2 * i * e + (INV % NA) * b * f), NA)
    row = lax.broadcasted_iota(jnp.int32, (LANES, LANES), 0)
    lane = lax.broadcasted_iota(jnp.int32, (LANES, LANES), 1)
    q, r = row // 64, row % 64
    q2, r2 = lane // 64, lane % 64
    lane_dft = turns(
        -(128 * r2 * r + ((4096 * INV) % NA) * q2 * q + 16 * r2 * e + ((64 * INV) % NA) * q2 * f), NA
    )
    return chirp, twist, jnp.concatenate(lane_dft, axis=1)


def band(taps, offset):
    hit = offset[..., None] == lax.broadcasted_iota(jnp.int32, (1,) * offset.ndim + (taps.shape[0],), offset.ndim)
    return jnp.sum(jnp.where(hit, taps, 0.0), axis=-1)


def clutter_tables(pulse, beam, eh):
    half = (pulse.shape[0] - 1) // 2
    row = lax.broadcasted_iota(jnp.int32, (BOT, BOT), 0)
    col = lax.broadcasted_iota(jnp.int32, (BOT, BOT), 1)
    adjoint = band(pulse, row - col + half)
    own = lax.dynamic_slice_in_dim(adjoint, 16 * eh, 16, 0)
    moved = adjoint.reshape(16, 8, BOT).swapaxes(0, 1).reshape(BOT, BOT)
    range_pair = jnp.einsum("ir,hr->ih", own, moved, precision=HIGHEST)
    reach = (beam.shape[0] - 1) // 2
    row = lax.broadcasted_iota(jnp.int32, (3 * LANES, LANES), 0)
    col = lax.broadcasted_iota(jnp.int32, (3 * LANES, LANES), 1)
    block, inside = row // LANES, row % LANES
    at = jnp.where(block == 0, inside - 16, jnp.where(block == 1, inside, inside + LANES))
    valid = (block == 1) | (inside < 16)
    beam_mix = band(beam, jnp.where(valid, col - at + reach, -1))
    taps = beam.shape[0]
    first = lax.broadcasted_iota(jnp.int32, (taps, 2 * taps - 1), 0)
    shift = lax.broadcasted_iota(jnp.int32, (taps, 2 * taps - 1), 1) - (taps - 1)
    auto = jnp.sum(beam[:, None] * band(beam, first + shift), axis=0)
    slot = lax.broadcasted_iota(jnp.int32, (3, LANES, LANES), 0)
    at = lax.broadcasted_iota(jnp.int32, (3, LANES, LANES), 1)
    col = lax.broadcasted_iota(jnp.int32, (3, LANES, LANES), 2)
    azimuth = jnp.where(slot < 2, at + 64 * slot, jnp.where(at < 32, at + LANES, at - 64))
    beam_pair = band(auto, jnp.where(at < 64, azimuth - col + taps - 1, -1))
    return adjoint, range_pair, beam_mix, beam_pair


VMEM = pl.BlockSpec(memory_space=pltpu.VMEM)
SMEM = pl.BlockSpec(memory_space=pltpu.SMEM)


def f32(*shape):
    return jax.ShapeDtypeStruct(shape, jnp.float32)


def call(kernel, outs, scratch, args, smem=False, cost=2_000_000, interpret=False):
    specs = [SMEM if smem and n == 0 else VMEM for n in range(len(args))]
    return pl.pallas_call(
        kernel,
        out_shape=outs,
        in_specs=specs,
        out_specs=jax.tree.map(lambda _: VMEM, outs),
        scratch_shapes=[pltpu.VMEM(shape, jnp.float32) for shape in scratch],
        cost_estimate=pl.CostEstimate(flops=cost * 100, bytes_accessed=cost, transcendentals=0),
        interpret=interpret,
    )(*args)


def stage_pack(place, field, terrain, pick, mask, measured, adjoint, **kw):
    turned = jnp.einsum("hr,sra->sha", adjoint, measured, precision=HIGHEST)
    args = (place, field, terrain[None], pick[None], mask, turned)
    return call(pack_kernel, f32(3 * ROWS, LANES), [], args, smem=True, **kw), turned


def stage_first(got, chirp, twist, lane_dft, **kw):
    args = (got, *chirp, *twist, lane_dft, jnp.asarray(SPLIT_DFT))
    scratch = [(2 * ROWS, LANES), (ROWS, LANES), (ROWS, LANES)]
    return call(first_kernel, f32(2 * ROWS, LANES), scratch, args, **kw)


def stage_prepare(place, got, profile, turned, beam_mix, chirp, **kw):
    outs = tuple(f32(ROWS, LANES) for _ in range(4)) + (f32(64, LANES), f32(2, 16, LANES))
    args = (place, got, profile, turned, beam_mix, *chirp)
    return call(prepare_kernel, outs, [(16, LANES)], args, smem=True, **kw)


def stage_middle(got, coef, both, twist, lane_dft, **kw):
    args = (got, *coef, *both, *twist, lane_dft, jnp.asarray(SPLIT_DFT), jnp.asarray(MIXED_DFT))
    scratch = [(2 * ROWS, LANES), (ROWS, LANES), (ROWS, LANES), (2 * ROWS, LANES)]
    return call(middle_kernel, (f32(2 * ROWS, LANES), f32(2, 64, LANES)), scratch, args, **kw)


def stage_last(place, got, coef, strip, seen, **kw):
    args = (place, got, *coef, strip, seen, jnp.asarray(PAIRS), jnp.asarray(MIXED_DFT))
    scratch = [(2 * ROWS, LANES), (64, LANES), (64, LANES)]
    return call(last_kernel, f32(3 * ROWS, LANES), scratch, args, smem=True, **kw)


def stage_unpack(place, got, mask, back_measured, range_pair, beam_pair, **kw):
    outs = (f32(2, NH // PH, LANES), f32(2, 2, 16, LANES))
    args = (place, got, mask, back_measured, range_pair, beam_pair)
    return call(unpack_kernel, outs, [(8 * LANES, LANES)], args, smem=True, **kw)


def swap(rows):
    width = rows.shape[0] // ROWS
    shaped = rows.reshape((ROWS, 2, LANES) if width == 2 else (ROWS, 1, width * LANES))
    moved = lax.all_to_all(shaped, ("ha", "az"), split_axis=0, concat_axis=0, tiled=True)
    return moved.reshape(rows.shape)


def local(field, terrain, profile_pick, profile_table, clutter_mask, pulse, beam, measured):
    e = lax.axis_index("ha")
    f = lax.axis_index("az")
    place = jnp.stack([e, f]).astype(jnp.int32)
    adjoint, range_pair, beam_mix, beam_pair = clutter_tables(pulse, beam, e)
    chirp, twist, lane_dft = layout_tables(e, f)
    sent, turned = stage_pack(place, field, terrain, profile_pick, clutter_mask, measured, adjoint)
    got = swap(sent)
    sent = stage_first(got, chirp, twist, lane_dft)
    prepared = stage_prepare(place, got, profile_table, turned, beam_mix, chirp)
    coef, both, seen, back_measured = prepared[0:2], prepared[2:4], prepared[4], prepared[5]
    got = swap(sent)
    sent, strip = stage_middle(got, coef, both, twist, lane_dft)
    got = swap(sent)
    sent = stage_last(place, got, coef, strip, seen)
    got = swap(sent)
    return stage_unpack(place, got, clutter_mask, back_measured, range_pair, beam_pair)


def solution(mesh):
    return jax.shard_map(
        local,
        mesh=mesh,
        in_specs=(
            P(None, "ha", "az"),
            P("az"),
            P("az"),
            P(),
            P(None, "az"),
            P(),
            P(),
            P(None, None, "az"),
        ),
        out_specs=(P(None, "ha", "az"), P(None, None, "ha", "az")),
        check_vma=False,
    )
```

```python
import functools
import math

import jax
import jax.numpy as jnp
import numpy as np
from jax import lax
from jax.experimental import pallas as pl
from jax.experimental.pallas import tpu as pltpu
from jax.sharding import PartitionSpec as P

NH, NA = 4096, 8192
PH, PA = 8, 64
ROWS = PH * PA
LANES = 128
BOT = 128
height_chirp = 1
azimuth_chirp = 3
INV = pow(azimuth_chirp, -1, 2 * NA)
HIGHEST = lax.Precision.HIGHEST
GRANT = 8 * 2**20


def gauss(count, spread):
    index = np.arange(count, dtype=np.int64)
    return np.sum(np.exp(-1j * np.pi * ((spread * index * index) % (2 * count)) / count)) / count


GAIN = gauss(NH, height_chirp) * gauss(NA, azimuth_chirp)


def row_matrices():
    turn = 2.0 * np.pi * ((INV * np.outer(np.arange(PA), np.arange(PA))) % PA) / PA
    re, im = np.cos(turn), -np.sin(turn)
    split = np.block([[re, -im], [im, re]])
    mixed = split.reshape(2 * PA, 2, PA).transpose(0, 2, 1).reshape(2 * PA, 2 * PA)
    return split.astype(np.float32), mixed.astype(np.float32)


def halves(value):
    high = value.astype(jnp.bfloat16)
    return high, (value - high.astype(jnp.float32)).astype(jnp.bfloat16)


def rounded_halves(value):
    high = lax.reduce_precision(value, 8, 7)
    return high.astype(jnp.bfloat16), (value - high).astype(jnp.bfloat16)


def matrix_left(value, split=rounded_halves):
    high, low = split(value)
    return jnp.concatenate([high, high, low], axis=1)


def matrix_right(value):
    high, low = rounded_halves(value)
    return jnp.concatenate([high, high, low], axis=0)


def data_left(value):
    high, low = halves(value)
    return jnp.concatenate([high, low, high], axis=1)


def data_right(value):
    high, low = halves(value)
    return jnp.concatenate([high, low, high], axis=0)


def product(left, right):
    return jnp.dot(left, right, preferred_element_type=jnp.float32)


SPLIT_DFT, MIXED_DFT = row_matrices()


def pair_choice():
    table = np.zeros((4, LANES, LANES), np.float32)
    for part in range(4):
        for q in range(2):
            for o in range(8):
                for j in range(2):
                    table[part, 64 * q + 2 * o + j, 16 * o + 2 * (2 * part + q) + j] = 1.0
    return table.reshape(4 * LANES, LANES)


PAIRS = pair_choice()


def dot(left, right):
    return jnp.dot(left, right, precision=HIGHEST, preferred_element_type=jnp.float32)


def lane_of(shape):
    return lax.broadcasted_iota(jnp.int32, shape, len(shape) - 1)


def row_of(shape):
    return lax.broadcasted_iota(jnp.int32, shape, len(shape) - 2)


def dft4(re, im):
    sr, si = re[0] + re[2], im[0] + im[2]
    dr, di = re[0] - re[2], im[0] - im[2]
    tr, ti = re[1] + re[3], im[1] + im[3]
    ur, ui = re[1] - re[3], im[1] - im[3]
    return [sr + tr, dr + ui, sr - tr, dr - ui], [si + ti, di - ur, si - ti, di + ur]


def dft8(re, im):
    half = math.sqrt(0.5)
    er, ei = dft4(re[0::2], im[0::2])
    pr, pi = dft4(re[1::2], im[1::2])
    tr = [pr[0], half * (pr[1] + pi[1]), pi[2], half * (pi[3] - pr[3])]
    ti = [pi[0], half * (pi[1] - pr[1]), -pr[2], -half * (pr[3] + pi[3])]
    out_re = [er[k] + tr[k] for k in range(4)] + [er[k] - tr[k] for k in range(4)]
    out_im = [ei[k] + ti[k] for k in range(4)] + [ei[k] - ti[k] for k in range(4)]
    return out_re, out_im


def dft8_group(held, group):
    low = 8 * group
    re = [held[i * 128 + low : i * 128 + low + 8, :] for i in range(8)]
    im = [held[i * 128 + 64 + low : i * 128 + 64 + low + 8, :] for i in range(8)]
    return dft8(re, im)


def flip_halves(block):
    turned = jnp.concatenate([block, block], axis=0).T
    return jnp.where(lane_of((64, LANES)) < 64, turned[:64], turned[64:])


def pack_kernel(place, field, terrain, pick, mask, measured, pulse, out, turned, taps):
    dh, da = place[0], place[1]
    taps[...] = jnp.zeros_like(taps)
    taps[:, 0 : pulse.shape[1]] = pulse[...]
    half = (pulse.shape[1] - 1) // 2
    wide = jnp.broadcast_to(taps[...], (BOT, 2 * LANES))
    adjoint = pltpu.roll(wide, 2 * LANES - half, 1, stride=1, stride_axis=0)[:, :LANES]
    both = jnp.concatenate([measured[0], measured[1]], axis=1)
    result = product(matrix_left(adjoint.T, halves), data_right(both))
    turned[0] = result[:, :LANES]
    turned[1] = result[:, LANES:]
    lanes = lane_of((64, LANES))
    rows = row_of((64, LANES))
    pads = [
        terrain[...].astype(jnp.float32),
        pick[...].astype(jnp.float32),
        jnp.zeros((14, LANES), jnp.float32),
        mask[pl.ds(pl.multiple_of(16 * dh, 16), 16), :].astype(jnp.float32),
    ]
    stacked = jnp.concatenate([jnp.zeros((64, LANES), jnp.float32)] + pads + pads, axis=0)
    upright = stacked.T
    common = jnp.where(lanes < 96, upright[:64], upright[64:])
    lane8 = lane_of((8, LANES))
    head = jnp.zeros((8, LANES), jnp.float32)
    tail = jnp.zeros((8, LANES), jnp.float32)
    for s in range(2):
        for j in range(2):
            slot = 2 * s + j
            part = turned.at[s][pl.ds(dh + 8 * j, 8, stride=16), :]
            here = (lane8 >= 16 * slot) & (lane8 < 16 * slot + 16)
            first = part if slot == 0 else pltpu.roll(part, 16 * slot, 1)
            head = jnp.where(here, first, head)
            tail = jnp.where(here, pltpu.roll(part, 16 + 16 * slot, 1), tail)
    right = lax.rem(da + 1, PA)
    left = lax.rem(da + PA - 1, PA)
    for e in range(8):
        spread_tail = jnp.broadcast_to(tail[e : e + 1, :], (64, LANES))
        spread_head = jnp.broadcast_to(head[e : e + 1, :], (64, LANES))
        edge = jnp.where(rows == right, spread_tail, jnp.where(rows == left, spread_head, 0.0))
        for c in range(2):
            out[pl.ds(e * 192 + c, 64, stride=3), :] = flip_halves(
                field.at[c][pl.ds(e, 64, stride=8), :]
            )
        out[pl.ds(e * 192 + 2, 64, stride=3), :] = jnp.where(lanes < 64, edge, common)


def finish_send(held, twist_re, twist_im, lane_dft, out, mid):
    for group in range(8):
        re, im = dft8_group(held, group)
        for k in range(8):
            at = slice(k * 64 + 8 * group, k * 64 + 8 * group + 8)
            tr, ti = twist_re[at, :], twist_im[at, :]
            mid[at, :LANES] = re[k] * tr - im[k] * ti
            mid[at, LANES:] = re[k] * ti + im[k] * tr
    result = product(data_left(mid[...]), lane_dft[...])
    out[pl.ds(0, ROWS, stride=2), :] = result[:, :LANES]
    out[pl.ds(1, ROWS, stride=2), :] = result[:, LANES:]


def row_dft(matrix, blocks, held):
    for i in range(0, 8, 2):
        pair = jnp.concatenate([blocks(i), blocks(i + 1)], axis=1)
        result = product(matrix[...], data_right(pair))
        held[i * 128 : (i + 1) * 128, :] = result[:, :LANES]
        held[(i + 1) * 128 : (i + 2) * 128, :] = result[:, LANES:]


def first_kernel(got, chirp_re, chirp_im, twist_re, twist_im, lane_dft, split, out, held, mid):
    def block(i):
        xr = got[pl.ds(i * 192, 64, stride=3), :]
        xi = got[pl.ds(i * 192 + 1, 64, stride=3), :]
        at = slice(i * 64, i * 64 + 64)
        dr, di = chirp_re[at, :], chirp_im[at, :]
        return jnp.concatenate([xr * dr - xi * di, xr * di + xi * dr], axis=0)

    row_dft(split, block, held)
    finish_send(held, twist_re, twist_im, lane_dft, out, mid)


def middle_kernel(
    got, coef_re, coef_im, both_re, both_im, twist_re, twist_im, lane_dft, split, mixed,
    out, strip, held, mid, next_in,
):
    row_dft(mixed, lambda i: got[i * 128 : (i + 1) * 128, :], held)
    for group in range(8):
        re, im = dft8_group(held, group)
        low = 8 * group
        cr, ci = coef_re[low : low + 8, :], coef_im[low : low + 8, :]
        strip[0, low : low + 8, :] = re[0] * cr - im[0] * ci
        strip[1, low : low + 8, :] = re[0] * ci + im[0] * cr
        for k in range(8):
            at = slice(k * 64 + low, k * 64 + low + 8)
            cr, ci = both_re[at, :], both_im[at, :]
            next_in[k * 128 + low : k * 128 + low + 8, :] = re[k] * cr - im[k] * ci
            next_in[k * 128 + 64 + low : k * 128 + 64 + low + 8, :] = re[k] * ci + im[k] * cr
    row_dft(split, lambda i: next_in[i * 128 : (i + 1) * 128, :], held)
    finish_send(held, twist_re, twist_im, lane_dft, out, mid)


def last_kernel(place, got, coef_re, coef_im, strip, seen, pairs, mixed, out, held, low_re, low_im):
    f = place[1]
    row_dft(mixed, lambda i: got[i * 128 : (i + 1) * 128, :], held)
    for group in range(8):
        re, im = dft8_group(held, group)
        low = 8 * group
        for k in range(8):
            at = slice(k * 64 + low, k * 64 + low + 8)
            cr, ci = coef_re[at, :], coef_im[at, :]
            new_re = re[k] * cr - im[k] * ci
            new_im = re[k] * ci + im[k] * cr
            out[pl.ds(3 * (k * 64 + low), 8, stride=3), :] = new_re
            out[pl.ds(3 * (k * 64 + low) + 1, 8, stride=3), :] = new_im
            if k == 0:
                low_re[low : low + 8, :] = new_re
                low_im[low : low + 8, :] = new_im
    lanes = lane_of((64, LANES))
    parts = [strip[0], strip[1], low_re[...], low_im[...]]
    high, low = halves(jnp.concatenate(parts, axis=1))
    chosen = product(high, pairs[...]) + product(low, pairs[...])
    powers = jnp.zeros((64, LANES), jnp.float32)
    for s in range(2):
        power = seen[...] * (parts[2 * s] * parts[2 * s] + parts[2 * s + 1] * parts[2 * s + 1])
        base = 48 * s
        after = pltpu.roll(power, PA - 1, 0)
        before = pltpu.roll(power, 1, 0)
        near = power if base == 0 else pltpu.roll(power, base, 1)
        other = pltpu.roll(power, base + 16 + 64, 1)
        side = jnp.where(
            f < 32, pltpu.roll(after, base + 32, 1), pltpu.roll(before, (base + 32 + 64) % LANES, 1)
        )
        for slot, moved in enumerate((near, other, side)):
            at = base + 16 * slot
            powers = jnp.where((lanes >= at) & (lanes < at + 16), moved, powers)
    for o in range(8):
        shift = (96 - 16 * o) % LANES
        moved = chosen if shift == 0 else pltpu.roll(chosen, shift, 1)
        out[pl.ds(o * 192 + 2, 64, stride=3), :] = jnp.where(lanes < 96, powers, moved)


def unpack_kernel(place, got, mask, back_measured, range_pair, beam_pair, field_out, sources, turned):
    eh = place[0]
    for e in range(8):
        for c in range(2):
            field_out.at[c][pl.ds(e, 64, stride=8), :] = flip_halves(
                got[pl.ds(e * 192 + c, 64, stride=3), :]
            )
        aux = got[pl.ds(e * 192 + 2, 64, stride=3), :]
        turned[e * 128 : (e + 1) * 128, :] = jnp.concatenate([aux, aux], axis=0).T
    seen = mask[pl.ds(pl.multiple_of(16 * eh, 16), 16), :].astype(jnp.float32)
    lane8 = lane_of((8, LANES))
    gathered = []
    for s in range(2):
        for slot in range(3):
            at = 48 * s + 16 * slot
            gathered.append(
                jnp.concatenate([turned[e * 128 + at : e * 128 + at + 16, :] for e in range(8)], axis=0)
            )
    ranged = product(range_pair[...], data_right(jnp.concatenate(gathered, axis=1)))
    ranged = jnp.concatenate([ranged[:, : 3 * LANES], ranged[:, 3 * LANES :]], axis=0)
    both_steps = product(data_left(ranged), beam_pair[...])
    for s in range(2):
        back = both_steps[16 * s : 16 * s + 16] - back_measured[s]
        for c in range(2):
            for j in range(2):
                at = 96 + 2 * (4 * s + 2 * c) + j
                near = turned[pl.ds(at, 8, stride=128), :]
                far = turned[pl.ds(at + 2, 8, stride=128), :]
                value = jnp.where(lane8 < 64, near, far)
                sources[s, c, 8 * j : 8 * j + 8, :] = (
                    2.0 * seen[8 * j : 8 * j + 8] * value * back[8 * j : 8 * j + 8]
                )


def prepare_kernel(
    place, got, profile, turned, beam_mix, chirp_re, chirp_im,
    coef_re, coef_im, both_re, both_im, seen, back_measured, edge,
):
    e, f = place[0], place[1]
    lanes = lane_of((64, LANES))
    rows = row_of((64, LANES))
    square = lane_of((LANES, LANES))
    down = row_of((LANES, LANES))
    total = jnp.zeros((64, LANES), jnp.float32)
    left = lax.rem(f + PA - 1, PA)
    right = lax.rem(f + 1, PA)
    first = got[pl.ds(2, 64, stride=3), :]
    for dh in range(8):
        aux = first if dh == 0 else got[pl.ds(dh * 192 + 2, 64, stride=3), :]
        j = lax.rem(square, 64) - 2 * dh
        wanted = 80 + 32 * (square // 64) + 8 * j + e
        choose = jnp.where((j >= 0) & (j < 2) & (down == wanted), 1.0, 0.0)
        total = total + jnp.dot(aux, choose, preferred_element_type=jnp.float32)
        edge[dh : dh + 1, :] = jnp.sum(jnp.where(rows == left, aux, 0.0), axis=0, keepdims=True)
        edge[8 + dh : 9 + dh, :] = jnp.sum(jnp.where(rows == right, aux, 0.0), axis=0, keepdims=True)
    seen[...] = total
    for s in range(2):
        for j in range(2):
            slot = 2 * s + j
            start = pl.multiple_of(16 * e + 8 * j, 8)
            own = dot(turned.at[s][pl.ds(start, 8), :], beam_mix[LANES : 2 * LANES, :])
            shift = (LANES - 16 * slot) % LANES
            near = edge[0:8, :] if shift == 0 else pltpu.roll(edge[0:8, :], shift, 1)
            far = edge[8:16, :] if shift == 0 else pltpu.roll(edge[8:16, :], shift, 1)
            own = own + dot(near, beam_mix[0:LANES, :])
            own = own + dot(far, beam_mix[2 * LANES : 3 * LANES, :])
            back_measured[s, 8 * j : 8 * j + 8, :] = own

    def column(lane):
        return jnp.sum(jnp.where(lanes == lane, first, 0.0), axis=1, keepdims=True)

    pick0, pick1 = column(65), column(97)
    onehot = jnp.where(lanes < 16, pick0, pick1 + 16.0) == lanes.astype(jnp.float32)
    onehot = jnp.where(onehot & (lanes < 32), 1.0, 0.0)
    ground = jnp.where(lanes < 64, column(64), column(96))
    tall = row_of((512, LANES))
    choose = jnp.where(tall == 8 * lax.rem(lane_of((512, LANES)), 64) + e, 1.0, 0.0)
    lane16 = lane_of((16, LANES))
    for i in range(8):
        phase = dot(profile[:, 512 * i : 512 * (i + 1)], choose)
        height = 512 * i + 8 * lax.rem(lane16, 64) + e
        depth = jnp.maximum(height.astype(jnp.float32) - 0.75 * NH, 0.0) / (0.25 * NH)
        amount = abs(GAIN) * jnp.exp(-4.0 * depth * depth)
        angle = phase + float(np.angle(GAIN))
        pair = []
        for value in (amount * jnp.cos(angle), amount * jnp.sin(angle)):
            lower = jnp.where(lane16 < 64, value, 0.0)
            upper = jnp.where(lane16 < 64, 0.0, value)
            pair.append(
                dot(onehot, jnp.concatenate([lower, upper, jnp.zeros((96, LANES), jnp.float32)], axis=0))
            )
        at = slice(i * 64, i * 64 + 64)
        above = (512 * i + 8 * lax.rem(lanes, 64) + e).astype(jnp.float32) >= ground
        sr = jnp.where(above, pair[0], 0.0)
        si = jnp.where(above, pair[1], 0.0)
        dr, di = chirp_re[at, :], chirp_im[at, :]
        cr, ci = sr * dr - si * di, sr * di + si * dr
        coef_re[at, :] = cr
        coef_im[at, :] = ci
        both_re[at, :] = cr * dr - ci * di
        both_im[at, :] = cr * di + ci * dr


def turns(steps, modulus):
    angle = (steps % modulus).astype(jnp.float32) * (2.0 * math.pi / modulus)
    return jnp.cos(angle), jnp.sin(angle)


def layout_tables(e, f):
    row = lax.broadcasted_iota(jnp.int32, (ROWS, LANES), 0)
    lane = lax.broadcasted_iota(jnp.int32, (ROWS, LANES), 1)
    i, b = row // PA, row % PA
    q, r = lane // 64, lane % 64
    square_h = 64 * r * r + e * e + 1024 * i * e + 16 * r * e
    square_a = INV * (4096 * q * q + f * f + 128 * q * f) + ((256 * INV) % (2 * NA)) * b * f
    chirp = turns(2 * square_h + square_a, 2 * NA)
    twist = turns(-(16 * i * r + ((64 * INV) % NA) * b * q + 2 * i * e + (INV % NA) * b * f), NA)
    row = lax.broadcasted_iota(jnp.int32, (LANES, LANES), 0)
    lane = lax.broadcasted_iota(jnp.int32, (LANES, LANES), 1)
    q, r = row // 64, row % 64
    q2, r2 = lane // 64, lane % 64
    lane_dft = turns(
        -(128 * r2 * r + ((4096 * INV) % NA) * q2 * q + 16 * r2 * e + ((64 * INV) % NA) * q2 * f), NA
    )
    re, im = lane_dft
    whole = jnp.concatenate([jnp.concatenate([re, im], axis=1), jnp.concatenate([-im, re], axis=1)], axis=0)
    return chirp, twist, matrix_right(whole)


def band(taps, offset):
    hit = offset[..., None] == lax.broadcasted_iota(jnp.int32, (1,) * offset.ndim + (taps.shape[0],), offset.ndim)
    return jnp.sum(jnp.where(hit, taps, 0.0), axis=-1)


def clutter_tables(pulse, beam, eh):
    half = (pulse.shape[0] - 1) // 2
    row = lax.broadcasted_iota(jnp.int32, (BOT, BOT), 0)
    col = lax.broadcasted_iota(jnp.int32, (BOT, BOT), 1)
    adjoint = band(pulse, row - col + half)
    own = lax.dynamic_slice_in_dim(adjoint, 16 * eh, 16, 0)
    moved = adjoint.reshape(16, 8, BOT).swapaxes(0, 1).reshape(BOT, BOT)
    range_pair = jnp.einsum("ir,hr->ih", own, moved, precision=HIGHEST)
    reach = (beam.shape[0] - 1) // 2
    row = lax.broadcasted_iota(jnp.int32, (3 * LANES, LANES), 0)
    col = lax.broadcasted_iota(jnp.int32, (3 * LANES, LANES), 1)
    block, inside = row // LANES, row % LANES
    at = jnp.where(block == 0, inside - 16, jnp.where(block == 1, inside, inside + LANES))
    valid = (block == 1) | (inside < 16)
    beam_mix = band(beam, jnp.where(valid, col - at + reach, -1))
    taps = beam.shape[0]
    first = lax.broadcasted_iota(jnp.int32, (taps, 2 * taps - 1), 0)
    shift = lax.broadcasted_iota(jnp.int32, (taps, 2 * taps - 1), 1) - (taps - 1)
    auto = jnp.sum(beam[:, None] * band(beam, first + shift), axis=0)
    slot = lax.broadcasted_iota(jnp.int32, (3, LANES, LANES), 0)
    at = lax.broadcasted_iota(jnp.int32, (3, LANES, LANES), 1)
    col = lax.broadcasted_iota(jnp.int32, (3, LANES, LANES), 2)
    azimuth = jnp.where(slot < 2, at + 64 * slot, jnp.where(at < 32, at + LANES, at - 64))
    beam_pair = band(auto, jnp.where(at < 64, azimuth - col + taps - 1, -1))
    return matrix_left(range_pair), beam_mix, matrix_right(beam_pair.reshape(3 * LANES, LANES))


VMEM = pl.BlockSpec(memory_space=pltpu.VMEM)
SMEM = pl.BlockSpec(memory_space=pltpu.SMEM)


def f32(*shape):
    return jax.ShapeDtypeStruct(shape, jnp.float32)


def placed(kernel, *refs):
    return kernel((lax.axis_index("ha"), lax.axis_index("az")), *refs)


def call(kernel, outs, scratch, args, place=None, cost=2_000_000, interpret=False):
    specs = [VMEM] * len(args)
    if place == "here":
        kernel = functools.partial(placed, kernel)
    elif place is not None:
        specs, args = [SMEM] + specs, (place, *args)
    return pl.pallas_call(
        kernel,
        out_shape=outs,
        in_specs=specs,
        out_specs=jax.tree.map(lambda _: VMEM, outs),
        scratch_shapes=[pltpu.VMEM(shape, jnp.float32) for shape in scratch],
        cost_estimate=pl.CostEstimate(flops=cost * 100, bytes_accessed=cost, transcendentals=0),
        compiler_params=pltpu.CompilerParams(vmem_limit_bytes=GRANT),
        interpret=interpret,
    )(*args)


def split_matrix():
    return matrix_left(jnp.asarray(SPLIT_DFT))


def mixed_matrix():
    return matrix_left(jnp.asarray(MIXED_DFT))


def stage_pack(place, field, terrain, pick, mask, measured, pulse, **kw):
    args = (field, terrain[None], pick[None], mask, measured, pulse[None])
    outs = (f32(3 * ROWS, LANES), f32(2, BOT, LANES))
    return call(pack_kernel, outs, [(1, 2 * LANES)], args, place, **kw)


def stage_first(got, chirp, twist, lane_dft, **kw):
    args = (got, *chirp, *twist, lane_dft, split_matrix())
    scratch = [(2 * ROWS, LANES), (ROWS, 2 * LANES)]
    return call(first_kernel, f32(2 * ROWS, LANES), scratch, args, **kw)


def stage_prepare(place, got, profile, turned, beam_mix, chirp, **kw):
    outs = tuple(f32(ROWS, LANES) for _ in range(4)) + (f32(64, LANES), f32(2, 16, LANES))
    args = (got, profile, turned, beam_mix, *chirp)
    return call(prepare_kernel, outs, [(16, LANES)], args, place, **kw)


def stage_middle(got, coef, both, twist, lane_dft, **kw):
    args = (got, *coef, *both, *twist, lane_dft, split_matrix(), mixed_matrix())
    scratch = [(2 * ROWS, LANES), (ROWS, 2 * LANES), (2 * ROWS, LANES)]
    return call(middle_kernel, (f32(2 * ROWS, LANES), f32(2, 64, LANES)), scratch, args, **kw)


def stage_last(place, got, coef, strip, seen, **kw):
    args = (got, *coef, strip, seen, jnp.asarray(PAIRS).astype(jnp.bfloat16), mixed_matrix())
    scratch = [(2 * ROWS, LANES), (64, LANES), (64, LANES)]
    return call(last_kernel, f32(3 * ROWS, LANES), scratch, args, place, **kw)


def stage_unpack(place, got, mask, back_measured, range_pair, beam_pair, **kw):
    outs = (f32(2, NH // PH, LANES), f32(2, 2, 16, LANES))
    args = (got, mask, back_measured, range_pair, beam_pair)
    return call(unpack_kernel, outs, [(8 * LANES, LANES)], args, place, **kw)


def swap(rows):
    width = rows.shape[0] // ROWS
    shaped = rows.reshape((ROWS, 2, LANES) if width == 2 else (ROWS, 1, width * LANES))
    moved = lax.all_to_all(shaped, ("ha", "az"), split_axis=0, concat_axis=0, tiled=True)
    return moved.reshape(rows.shape)


def local(field, terrain, profile_pick, profile_table, clutter_mask, pulse, beam, measured):
    e = lax.axis_index("ha")
    f = lax.axis_index("az")
    place = "here"
    range_pair, beam_mix, beam_pair = clutter_tables(pulse, beam, e)
    chirp, twist, lane_dft = layout_tables(e, f)
    sent, turned = stage_pack(place, field, terrain, profile_pick, clutter_mask, measured, pulse)
    got = swap(sent)
    sent = stage_first(got, chirp, twist, lane_dft)
    prepared = stage_prepare(place, got, profile_table, turned, beam_mix, chirp)
    coef, both, seen, back_measured = prepared[0:2], prepared[2:4], prepared[4], prepared[5]
    got = swap(sent)
    sent, strip = stage_middle(got, coef, both, twist, lane_dft)
    got = swap(sent)
    sent = stage_last(place, got, coef, strip, seen)
    got = swap(sent)
    return stage_unpack(place, got, clutter_mask, back_measured, range_pair, beam_pair)


def solution(mesh):
    return jax.shard_map(
        local,
        mesh=mesh,
        in_specs=(
            P(None, "ha", "az"),
            P("az"),
            P("az"),
            P(),
            P(None, "az"),
            P(),
            P(),
            P(None, None, "az"),
        ),
        out_specs=(P(None, "ha", "az"), P(None, None, "ha", "az")),
        check_vma=False,
    )
```

```python
import functools
import math

import jax
import jax.numpy as jnp
import numpy as np
from jax import lax
from jax.experimental import pallas as pl
from jax.experimental.pallas import tpu as pltpu
from jax.sharding import PartitionSpec as P

NH, NA = 4096, 8192
PH, PA = 8, 64
ROWS = PH * PA
LANES = 128
BOT = 128
PART = 144
height_chirp = 1
azimuth_chirp = 3
INV = pow(azimuth_chirp, -1, 2 * NA)
HIGHEST = lax.Precision.HIGHEST
GRANT = 8 * 2**20
WIDE_GRANT = 60 * 2**20


def gauss(count, spread):
    index = np.arange(count, dtype=np.int64)
    return np.sum(np.exp(-1j * np.pi * ((spread * index * index) % (2 * count)) / count)) / count


GAIN = gauss(NH, height_chirp) * gauss(NA, azimuth_chirp)


def halves(value):
    high = value.astype(jnp.bfloat16)
    return high, (value - high.astype(jnp.float32)).astype(jnp.bfloat16)


def rounded_halves(value):
    high = lax.reduce_precision(value, 8, 7)
    return high.astype(jnp.bfloat16), (value - high).astype(jnp.bfloat16)


def matrix_left(value):
    high, low = rounded_halves(value)
    return jnp.concatenate([high, high, low], axis=1)


def matrix_right(value):
    high, low = rounded_halves(value)
    return jnp.concatenate([high, high, low], axis=0)


def data_left(value):
    high, low = halves(value)
    return jnp.concatenate([high, low, high], axis=1)


def data_right(value):
    high, low = halves(value)
    return jnp.concatenate([high, low, high], axis=0)


def product(left, right):
    return jnp.dot(left, right, preferred_element_type=jnp.float32)


def dot(left, right):
    return jnp.dot(left, right, precision=HIGHEST, preferred_element_type=jnp.float32)


def roots(count, spread):
    index = np.arange(count)
    return np.exp(-2j * np.pi * ((spread * np.outer(index, index)) % count) / count)


def row_matrix(spread):
    table = roots(PA, spread)
    whole = np.block([[table.real, -table.imag], [table.imag, table.real]]).astype(np.float32)
    return matrix_left(jnp.asarray(whole))


def lane_matrix(table):
    whole = np.block([[table.real, table.imag], [-table.imag, table.real]]).astype(np.float32)
    return matrix_right(jnp.asarray(whole))


def height_lanes():
    return lane_matrix(np.kron(roots(8, 1), np.eye(16)))


def azimuth_lanes():
    return lane_matrix(np.kron(np.eye(8), roots(16, INV)))


def tiles():
    table = np.zeros((LANES, 4, 8, 16), np.float32)
    for o in range(4):
        for k in range(16):
            table[16 * o + k, o, :, k] = 1.0
    return jnp.asarray(table.reshape(LANES, 4 * LANES)).astype(jnp.bfloat16)


def lane_of(shape):
    return lax.broadcasted_iota(jnp.int32, shape, len(shape) - 1)


def row_of(shape):
    return lax.broadcasted_iota(jnp.int32, shape, len(shape) - 2)


def cmul(ar, ai, br, bi):
    return ar * br - ai * bi, ar * bi + ai * br


def dft4(re, im):
    sr, si = re[0] + re[2], im[0] + im[2]
    dr, di = re[0] - re[2], im[0] - im[2]
    tr, ti = re[1] + re[3], im[1] + im[3]
    ur, ui = re[1] - re[3], im[1] - im[3]
    return [sr + tr, dr + ui, sr - tr, dr - ui], [si + ti, di - ur, si - ti, di + ur]


def dft8(re, im):
    half = math.sqrt(0.5)
    er, ei = dft4(re[0::2], im[0::2])
    pr, pi = dft4(re[1::2], im[1::2])
    tr = [pr[0], half * (pr[1] + pi[1]), pi[2], half * (pi[3] - pr[3])]
    ti = [pi[0], half * (pi[1] - pr[1]), -pr[2], -half * (pr[3] + pi[3])]
    out_re = [er[k] + tr[k] for k in range(4)] + [er[k] - tr[k] for k in range(4)]
    out_im = [ei[k] + ti[k] for k in range(4)] + [ei[k] - ti[k] for k in range(4)]
    return out_re, out_im


def dft8_azimuth(re, im):
    out_re, out_im = dft8(re, im)
    order = [(INV * k) % 8 for k in range(8)]
    return [out_re[k] for k in order], [out_im[k] for k in order]


def shift(value, amount):
    amount = amount % LANES
    return value if amount == 0 else pltpu.roll(value, amount, 1)


def trade(parts):
    group = lane_of(parts[0].shape) // 16
    parts = list(parts)
    for bit in (1, 2, 4):
        keep = (group & bit) == 0
        for a in range(8):
            if a & bit == 0:
                low, high = parts[a], parts[a | bit]
                parts[a] = jnp.where(keep, low, shift(high, 16 * bit))
                parts[a | bit] = jnp.where(keep, shift(low, -16 * bit), high)
    return parts


def row_dft(matrix, source, held):
    for i in range(0, 8, 2):
        pair = jnp.concatenate([source(i), source(i + 1)], axis=1)
        result = product(matrix[...], data_right(pair))
        held[i * 128 : (i + 1) * 128, :] = result[:, :LANES]
        held[(i + 1) * 128 : (i + 2) * 128, :] = result[:, LANES:]


def block_of(ref):
    return lambda i: ref[i * 128 : (i + 1) * 128, :]


def re_rows(i, low):
    return slice(i * 128 + low, i * 128 + low + 8)


def im_rows(i, low):
    return slice(i * 128 + 64 + low, i * 128 + 64 + low + 8)


def flat_rows(i, low):
    return slice(i * 64 + low, i * 64 + low + 8)


def pack_kernel(field, out):
    for c in range(2):
        for part in range(8):
            rows = [field.at[c][pl.ds(64 * part + g, 8, stride=8), :] for g in range(8)]
            for e, value in enumerate(trade(rows)):
                at = e * 128 + c * 64 + 8 * part
                out[at : at + 8, :] = value


def columns_kernel(
    place, got, chirp_re, chirp_im, outer_re, outer_im, inner_re, inner_im, last_re, last_im, split, lanes_dft,
    pick, terrain, out, work, held, mid,
):
    e = place[0]
    for group in range(8):
        low = 8 * group
        re, im = [], []
        for i in range(8):
            at = flat_rows(i, low)
            r, m = cmul(got[re_rows(i, low), :], got[im_rows(i, low), :], chirp_re[at, :], chirp_im[at, :])
            re.append(r)
            im.append(m)
        re, im = dft8(re, im)
        for i in range(8):
            at = flat_rows(i, low)
            r, m = cmul(re[i], im[i], outer_re[at, :], outer_im[at, :])
            work[re_rows(i, low), :] = r
            work[im_rows(i, low), :] = m
    row_dft(split, block_of(work), held)
    ir, ii = inner_re[...], inner_im[...]
    for i in range(8):
        at = slice(i * 64, i * 64 + 64)
        r, m = cmul(held[i * 128 : i * 128 + 64, :], held[i * 128 + 64 : i * 128 + 128, :], ir, ii)
        mid[at, :LANES] = r
        mid[at, LANES:] = m
    result = product(data_left(mid[...]), lanes_dft[...])
    r, m = cmul(result[:, :LANES], result[:, LANES:], last_re[...], last_im[...])
    out[pl.ds(0, ROWS, stride=3), :] = r
    out[pl.ds(1, ROWS, stride=3), :] = m
    lane8 = lane_of((8, LANES))
    picks = pltpu.roll(jnp.broadcast_to(pick[...].astype(jnp.float32), (8, LANES)), LANES - 16 * e, 1)
    lows = pltpu.roll(
        jnp.broadcast_to(terrain[...].astype(jnp.float32), (8, LANES)), lax.rem(LANES + 16 - 16 * e, LANES), 1
    )
    aux = jnp.where(lane8 < 16, picks, jnp.where(lane8 < 32, lows, 0.0))
    out[pl.ds(2, ROWS, stride=3), :] = jnp.broadcast_to(aux[None], (PA, 8, LANES)).reshape(ROWS, LANES)


def select_profile(picks, table):
    bits = picks.astype(jnp.int32)
    level = [table[p : p + 1, :] for p in range(16)]
    for bit in (1, 2, 4, 8):
        test = (bits & bit) != 0
        level = [jnp.where(test, level[k + 1], level[k]) for k in range(0, len(level), 2)]
    return level[0]


def rows_kernel(
    place, got, chirp_re, chirp_im, outer_re, outer_im, inner_re, inner_im, back_re, back_im, split, lanes_dft,
    tile, screen_re, screen_im, out, work, held, mid, picks, lows, low_strip,
):
    e, f = place[0], place[1]

    def chirped(i):
        at = slice(i * 64, i * 64 + 64)
        r, m = cmul(
            got[pl.ds(i * 192, 64, stride=3), :],
            got[pl.ds(i * 192 + 1, 64, stride=3), :],
            chirp_re[at, :],
            chirp_im[at, :],
        )
        return jnp.concatenate([r, m], axis=0)

    row_dft(split, chirped, held)
    for i in range(8):
        parts = [got[pl.ds(i * 192 + 2 + 3 * o, 16, stride=12), :] for o in range(4)]
        upright = jnp.concatenate(parts + parts, axis=0).T
        spread = product(upright[:32].astype(jnp.bfloat16), tile[...])
        for o in range(4):
            at = (i // 4 + 2 * o) * 64 + 16 * (i % 4)
            picks[at : at + 16, :] = spread[:16, o * LANES : (o + 1) * LANES]
            lows[at : at + 16, :] = spread[16:, o * LANES : (o + 1) * LANES]
    for group in range(8):
        low = 8 * group
        re, im = [], []
        for i in range(8):
            at = flat_rows(i, low)
            r, m = cmul(held[re_rows(i, low), :], held[im_rows(i, low), :], outer_re[at, :], outer_im[at, :])
            re.append(r)
            im.append(m)
        re, im = dft8_azimuth(re, im)
        for i in range(8):
            r, m = cmul(re[i], im[i], inner_re[i : i + 1, :], inner_im[i : i + 1, :])
            mid[flat_rows(i, low), :LANES] = r
            mid[flat_rows(i, low), LANES:] = m
    result = product(data_left(mid[...]), lanes_dft[...])
    lane8 = lane_of((8, LANES))
    height = (e + 8 * f + 512 * (lane8 // 16)).astype(jnp.float32)
    for n in range(0, ROWS, 8):
        at = slice(n, n + 8)
        above = height >= lows[at, :]
        sr = jnp.where(above, select_profile(picks[at, :], screen_re), 0.0)
        si = jnp.where(above, select_profile(picks[at, :], screen_im), 0.0)
        br, bi = back_re[at, :], back_im[at, :]
        r, m = cmul(sr, si, br, bi)
        r, m = cmul(result[at, :LANES], result[at, LANES:], r, m)
        low_strip[at, :] = jnp.where(lane8 < 16, r, shift(m, 16))
        r, m = cmul(r, m, br, bi)
        mid[at, :LANES] = r
        mid[at, LANES:] = m
    result = product(data_left(mid[...]), lanes_dft[...])
    for group in range(8):
        low = 8 * group
        re, im = [], []
        for i in range(8):
            at = flat_rows(i, low)
            r, m = cmul(result[at, :LANES], result[at, LANES:], inner_re[i : i + 1, :], inner_im[i : i + 1, :])
            re.append(r)
            im.append(m)
        re, im = dft8_azimuth(re, im)
        for i in range(8):
            at = flat_rows(i, low)
            r, m = cmul(re[i], im[i], outer_re[at, :], outer_im[at, :])
            work[re_rows(i, low), :] = r
            work[im_rows(i, low), :] = m
    row_dft(split, block_of(work), held)
    for i in range(8):
        at = slice(i * 64, i * 64 + 64)
        r, m = cmul(
            held[i * 128 : i * 128 + 64, :], held[i * 128 + 64 : i * 128 + 128, :], chirp_re[at, :], chirp_im[at, :]
        )
        out[pl.ds(i * 192, 64, stride=3), :] = r
        out[pl.ds(i * 192 + 1, 64, stride=3), :] = m
    lane16 = lane_of((16, LANES))
    for i in range(8):
        block = low_strip[i * 64 : i * 64 + 64, :]
        upright = jnp.concatenate([block, block], axis=0).T
        for part in range(4):
            re = shift(upright[:16], -16 * part)
            im = shift(upright[16:32], 16 - 16 * part)
            to = 4 * (i % 2) + part
            out[pl.ds(to * 192 + 2 + 3 * (i // 2), 16, stride=12), :] = jnp.where(
                lane16 < 16, re, jnp.where(lane16 < 32, im, 0.0)
            )


def final_kernel(
    got, chirp_re, chirp_im, outer_re, outer_im, inner_re, inner_im, coef_re, coef_im, split, lanes_dft,
    seen, range_pair, out, work, held, mid,
):
    for i in range(8):
        at = slice(i * 64, i * 64 + 64)
        r, m = cmul(
            got[pl.ds(i * 192, 64, stride=3), :],
            got[pl.ds(i * 192 + 1, 64, stride=3), :],
            chirp_re[at, :],
            chirp_im[at, :],
        )
        mid[at, :LANES] = r
        mid[at, LANES:] = m
    result = product(data_left(mid[...]), lanes_dft[...])
    ir, ii = inner_re[...], inner_im[...]
    for i in range(8):
        at = slice(i * 64, i * 64 + 64)
        r, m = cmul(result[at, :LANES], result[at, LANES:], ir, ii)
        work[i * 128 : i * 128 + 64, :] = r
        work[i * 128 + 64 : i * 128 + 128, :] = m
    row_dft(split, block_of(work), held)
    strip_re, strip_im = [], []
    for group in range(8):
        low = 8 * group
        re, im = [], []
        for i in range(8):
            at = flat_rows(i, low)
            r, m = cmul(held[re_rows(i, low), :], held[im_rows(i, low), :], outer_re[at, :], outer_im[at, :])
            re.append(r)
            im.append(m)
        re, im = dft8(re, im)
        for i in range(8):
            at = flat_rows(i, low)
            r, m = cmul(re[i], im[i], coef_re[at, :], coef_im[at, :])
            out[i * PART + low : i * PART + low + 8, :] = r
            out[i * PART + 64 + low : i * PART + 64 + low + 8, :] = m
            if i == 0 and group < 2:
                strip_re.append(r)
                strip_im.append(m)
    lane16 = lane_of((16, LANES))
    first_re = jnp.zeros((16, LANES), jnp.float32)
    first_im = jnp.zeros((16, LANES), jnp.float32)
    for i in range(8):
        aux = got[pl.ds(i * 192 + 2, 16, stride=3), :]
        here = lane16 // 16 == i
        first_re = jnp.where(here, shift(aux, 16 * i), first_re)
        first_im = jnp.where(here, shift(aux, 16 * i - 16), first_im)
    parts = [(first_re, first_im), (jnp.concatenate(strip_re, axis=0), jnp.concatenate(strip_im, axis=0))]
    power = [seen[...] * (re * re + im * im) for re, im in parts]
    tall = []
    for g in range(8):
        second = jnp.where(lane16 < 32, shift(power[1], 16 - 16 * g), 0.0)
        tall.append(jnp.where(lane16 < 16, shift(power[0], -16 * g), second))
    ranged = product(range_pair[...], data_right(jnp.concatenate(tall, axis=0)))
    for s in range(2):
        spread = jnp.zeros((16, LANES), jnp.float32)
        for g in range(8):
            moved = shift(ranged[16 * g : 16 * g + 16, :], 16 * g - 16 * s)
            spread = jnp.where(lane16 // 16 == g, moved, spread)
        for n, value in enumerate((spread, *parts[s])):
            for i in range(8):
                at = i * PART + 128 + 2 * (3 * s + n)
                out[at : at + 2, :] = value[2 * i : 2 * i + 2, :]
    for i in range(8):
        out[i * PART + 140 : i * PART + 144, :] = jnp.zeros((4, LANES), jnp.float32)


def strips_kernel(got, measured, edges, strips, rows):
    parts = [got[e * PART + 128 : e * PART + 144, :] for e in range(8)]
    for g, value in enumerate(trade(parts)):
        rows[pl.ds(g, 16, stride=8), :] = value
    for s in range(2):
        edges[16 * s : 16 * s + 16, :] = rows[48 * s : 48 * s + 16, :]
        edges[32 + 16 * s : 48 + 16 * s, :] = measured[s]
        strips[32 * s : 32 * s + 32, :] = rows[48 * s + 16 : 48 * s + 48, :]


def unpack_kernel(got, field_out):
    for c in range(2):
        for part in range(8):
            at = c * 64 + 8 * part
            values = trade([got[e * PART + at : e * PART + at + 8, :] for e in range(8)])
            for g, value in enumerate(values):
                field_out.at[c][pl.ds(64 * part + g, 8, stride=8), :] = value


def sources_kernel(place, left, own, right, strips, mask, beams, sources):
    near = jnp.concatenate([left[:32, :], own[:32, :], right[:32, :]], axis=1)
    far = jnp.concatenate([left[32:, :], own[32:, :], right[32:, :]], axis=1)
    back = product(data_left(jnp.concatenate([near, far], axis=1)), beams[...])
    seen = mask[pl.ds(pl.multiple_of(16 * place[0], 16), 16), :].astype(jnp.float32)
    for s in range(2):
        for c in range(2):
            at = 32 * s + 16 * c
            sources[s, c] = 2.0 * seen * strips[at : at + 16, :] * back[16 * s : 16 * s + 16, :]


def prepare_kernel(
    place, profile, pick, terrain, mask, chirp_re, chirp_im, screen_re, screen_im, coef_re, coef_im, seen, turned,
):
    e, f = place[0], place[1]
    lane16 = lane_of((16, LANES))
    group = lane16 // 16
    wide = lane_of((16, 512))
    phase = jnp.zeros((16, LANES), jnp.float32)
    for g in range(8):
        chosen = jnp.where(wide == e + 8 * f, profile[:, 512 * g : 512 * (g + 1)], 0.0)
        phase = jnp.where(group == g, jnp.sum(chosen, axis=1, keepdims=True), phase)

    def screen(height, angle):
        depth = jnp.maximum(height.astype(jnp.float32) - 0.75 * NH, 0.0) / (0.25 * NH)
        amount = abs(GAIN) * jnp.exp(-4.0 * depth * depth)
        turn = angle + float(np.angle(GAIN))
        return amount * jnp.cos(turn), amount * jnp.sin(turn)

    sr, si = screen(e + 8 * f + 512 * group, phase)
    screen_re[...] = sr
    screen_im[...] = si
    picks = jnp.zeros((8, LANES), jnp.float32)
    lows = jnp.zeros((8, LANES), jnp.float32)
    masks = jnp.zeros((16, LANES), jnp.float32)
    group8 = lane_of((8, LANES)) // 16
    wide_pick = jnp.broadcast_to(pick[...].astype(jnp.float32), (8, LANES))
    wide_low = jnp.broadcast_to(terrain[...].astype(jnp.float32), (8, LANES))
    for g in range(8):
        amount = lax.rem(LANES + 16 * g - 16 * e, LANES)
        picks = jnp.where(group8 == g, pltpu.roll(wide_pick, amount, 1), picks)
        lows = jnp.where(group8 == g, pltpu.roll(wide_low, amount, 1), lows)
        part = mask[pl.ds(g, 16, stride=8), :].astype(jnp.float32)
        masks = jnp.where(group == g, pltpu.roll(part, amount, 1), masks)
    seen[...] = masks
    square_row = row_of((LANES, LANES))
    square_lane = lane_of((LANES, LANES))
    wanted = jnp.broadcast_to(picks[0:1, :], (LANES, LANES))
    match = ((square_row % 16).astype(jnp.float32) == wanted) & (square_row // 16 == square_lane // 16)
    onehot = jnp.where(match, 1.0, 0.0)
    for n in range(NH // LANES):
        block = profile[:, LANES * n : LANES * (n + 1)]
        turned[LANES * n : LANES * (n + 1), :] = jnp.concatenate([block] * 8, axis=0).T
    lanes = lane_of((64, LANES))
    rows = row_of((64, LANES))
    for i in range(8):
        mixed = jnp.zeros((64, LANES), jnp.float32)
        for g in range(8):
            mixed = jnp.where(lanes // 16 == g, turned[pl.ds(512 * i + g, 64, stride=8), :], mixed)
        height = 512 * i + 8 * rows + lanes // 16
        sr, si = screen(height, dot(mixed, onehot))
        above = height.astype(jnp.float32) >= jnp.broadcast_to(lows[0:1, :], (64, LANES))
        at = slice(i * 64, i * 64 + 64)
        r, m = cmul(jnp.where(above, sr, 0.0), jnp.where(above, si, 0.0), chirp_re[at, :], chirp_im[at, :])
        coef_re[at, :] = r
        coef_im[at, :] = m


def turns(steps, modulus):
    angle = (steps % modulus).astype(jnp.float32) * (2.0 * math.pi / modulus)
    return jnp.cos(angle), jnp.sin(angle)


def layout_tables():
    row = lax.broadcasted_iota(jnp.int32, (ROWS, LANES), 0)
    lane = lax.broadcasted_iota(jnp.int32, (ROWS, LANES), 1)
    i, j, g, t = row // PA, row % PA, lane // 16, lane % 16
    square_row = lax.broadcasted_iota(jnp.int32, (PA, LANES), 0)
    group = lax.broadcasted_iota(jnp.int32, (PA, LANES), 1) // 16
    block = lax.broadcasted_iota(jnp.int32, (8, LANES), 0)
    inside = lax.broadcasted_iota(jnp.int32, (8, LANES), 1) % 16
    heights = (
        turns(64 * j * j + g * g + 1024 * i * g + 16 * j * g, 2 * NH),
        turns(-i * (8 * j + g), NH),
        turns(-square_row * group, 512),
        turns(i * i + 64 * j * j + 16 * i * j + 1024 * i * g, 2 * NH),
    )
    natural = (256 * i * i + t * t + 4096 * i * j + 256 * j * t + 32 * i * t) % (2 * NA)
    reverse = (j * j + 4096 * i * i + 128 * i * j + 1024 * j * t) % (2 * NA)
    azimuths = (
        turns(INV * natural, 2 * NA),
        turns(-(INV % NA) * (j * (16 * i + t)), NA),
        turns(-(INV % 128) * block * inside, 128),
        turns(INV * reverse, 2 * NA),
    )
    return heights, azimuths


def band(taps, offset):
    hit = offset[..., None] == lax.broadcasted_iota(jnp.int32, (1,) * offset.ndim + (taps.shape[0],), offset.ndim)
    return jnp.sum(jnp.where(hit, taps, 0.0), axis=-1)


def clutter_tables(pulse, beam, measured, eh):
    half = (pulse.shape[0] - 1) // 2
    row = lax.broadcasted_iota(jnp.int32, (BOT, BOT), 0)
    col = lax.broadcasted_iota(jnp.int32, (BOT, BOT), 1)
    adjoint = band(pulse, row - col + half)
    moved = adjoint.reshape(16, 8, BOT).swapaxes(0, 1).reshape(BOT, BOT)
    range_pair = jnp.einsum("ir,hr->ih", moved, moved, precision=HIGHEST)
    own = lax.dynamic_slice_in_dim(adjoint, 16 * eh, 16, 0)
    turned = jnp.einsum("hr,sra->sha", own, measured, precision=HIGHEST)
    taps = beam.shape[0]
    reach = (taps - 1) // 2
    at = lax.broadcasted_iota(jnp.int32, (3 * LANES, LANES), 0) - LANES
    col = lax.broadcasted_iota(jnp.int32, (3 * LANES, LANES), 1)
    first = lax.broadcasted_iota(jnp.int32, (taps, 2 * taps - 1), 0)
    ahead = lax.broadcasted_iota(jnp.int32, (taps, 2 * taps - 1), 1) - (taps - 1)
    auto = jnp.sum(beam[:, None] * band(beam, first + ahead), axis=0)
    pair = band(auto, at - col + taps - 1)
    back = band(beam, col - at + reach)
    return matrix_left(range_pair), turned, matrix_right(jnp.concatenate([pair, -back], axis=0))


VMEM = pl.BlockSpec(memory_space=pltpu.VMEM)
SMEM = pl.BlockSpec(memory_space=pltpu.SMEM)


def f32(*shape):
    return jax.ShapeDtypeStruct(shape, jnp.float32)


def placed(kernel, *refs):
    return kernel((lax.axis_index("ha"), lax.axis_index("az")), *refs)


def call(kernel, outs, scratch, args, place=None, cost=2_000_000, grant=GRANT, interpret=False):
    specs = [VMEM] * len(args)
    if place == "here":
        kernel = functools.partial(placed, kernel)
    elif place is not None:
        specs, args = [SMEM] + specs, (place, *args)
    return pl.pallas_call(
        kernel,
        out_shape=outs,
        in_specs=specs,
        out_specs=jax.tree.map(lambda _: VMEM, outs),
        scratch_shapes=[pltpu.VMEM(shape, jnp.float32) for shape in scratch],
        cost_estimate=pl.CostEstimate(flops=cost * 100, bytes_accessed=cost, transcendentals=0),
        compiler_params=pltpu.CompilerParams(vmem_limit_bytes=grant),
        interpret=interpret,
    )(*args)


WORK = [(2 * ROWS, LANES), (2 * ROWS, LANES), (ROWS, 2 * LANES)]


def stage_pack(field, **kw):
    return call(pack_kernel, f32(2 * ROWS, LANES), [], (field,), grant=WIDE_GRANT, **kw)


def stage_columns(place, got, heights, pick, terrain, **kw):
    chirp, outer, inner, last = heights
    args = (got, *chirp, *outer, *inner, *last, row_matrix(1), height_lanes(), pick[None], terrain[None])
    return call(columns_kernel, f32(3 * ROWS, LANES), WORK, args, place, **kw)


def stage_rows(place, got, azimuths, screen, **kw):
    chirp, outer, inner, back = azimuths
    args = (got, *chirp, *outer, *inner, *back, row_matrix(INV), azimuth_lanes(), tiles(), *screen)
    return call(rows_kernel, f32(3 * ROWS, LANES), WORK + [(ROWS, LANES)] * 3, args, place, **kw)


def stage_final(got, heights, coef, seen, range_pair, **kw):
    _, outer, inner, chirp = heights
    args = (got, *chirp, *outer, *inner, *coef, row_matrix(1), height_lanes(), seen, range_pair)
    return call(final_kernel, f32(8 * PART, LANES), WORK, args, **kw)


def stage_strips(got, turned, **kw):
    return call(strips_kernel, (f32(64, LANES), f32(64, LANES)), [(BOT, LANES)], (got, turned), **kw)


def stage_unpack(got, **kw):
    return call(unpack_kernel, f32(2, NH // PH, LANES), [], (got,), **kw)


def stage_sources(place, left, own, right, strips, mask, beams, **kw):
    return call(sources_kernel, f32(2, 2, 16, LANES), [], (left, own, right, strips, mask, beams), place, **kw)


def stage_prepare(place, profile, pick, terrain, mask, heights, **kw):
    outs = (f32(16, LANES), f32(16, LANES), f32(ROWS, LANES), f32(ROWS, LANES), f32(16, LANES))
    args = (profile, pick[None], terrain[None], mask, *heights[0])
    return call(prepare_kernel, outs, [(NH, LANES)], args, place, **kw)


def swap_all(rows):
    shaped = rows.reshape(ROWS, 1, 3 * LANES)
    moved = lax.all_to_all(shaped, ("ha", "az"), split_axis=0, concat_axis=0, tiled=True)
    return moved.reshape(rows.shape)


def swap_heights(rows):
    shaped = rows.reshape(PH, rows.shape[0] // PH, LANES)
    return lax.all_to_all(shaped, "ha", split_axis=0, concat_axis=0, tiled=True).reshape(rows.shape)


def local(field, terrain, profile_pick, profile_table, clutter_mask, pulse, beam, measured):
    place = "here"
    range_pair, turned, beams = clutter_tables(pulse, beam, measured, lax.axis_index("ha"))
    heights, azimuths = layout_tables()
    got = swap_heights(stage_pack(field))
    got = swap_all(stage_columns(place, got, heights, profile_pick, terrain))
    prepared = stage_prepare(place, profile_table, profile_pick, terrain, clutter_mask, heights)
    got = swap_all(stage_rows(place, got, azimuths, prepared[0:2]))
    got = swap_heights(stage_final(got, heights, prepared[2:4], prepared[4], range_pair))
    edges, strips = stage_strips(got, turned)
    left = lax.ppermute(edges, "az", [(i, (i + 1) % PA) for i in range(PA)])
    right = lax.ppermute(edges, "az", [((i + 1) % PA, i) for i in range(PA)])
    field_out = stage_unpack(got)
    return field_out, stage_sources(place, left, edges, right, strips, clutter_mask, beams)


def solution(mesh):
    return jax.shard_map(
        local,
        mesh=mesh,
        in_specs=(
            P(None, "ha", "az"),
            P("az"),
            P("az"),
            P(),
            P(None, "az"),
            P(),
            P(),
            P(None, None, "az"),
        ),
        out_specs=(P(None, "ha", "az"), P(None, None, "ha", "az")),
        check_vma=False,
    )
```

```python
import functools
import math

import jax
import jax.numpy as jnp
import numpy as np
from jax import lax
from jax.experimental import pallas as pl
from jax.experimental.pallas import tpu as pltpu
from jax.sharding import PartitionSpec as P

NH, NA = 4096, 8192
PH, PA = 8, 64
ROWS = PH * PA
LANES = 128
BOT = 128
PART = 144
height_chirp = 1
azimuth_chirp = 3
INV = pow(azimuth_chirp, -1, 2 * NA)
HIGHEST = lax.Precision.HIGHEST
GRANT = 8 * 2**20
WIDE_GRANT = 60 * 2**20


def gauss(count, spread):
    index = np.arange(count, dtype=np.int64)
    return np.sum(np.exp(-1j * np.pi * ((spread * index * index) % (2 * count)) / count)) / count


GAIN = gauss(NH, height_chirp) * gauss(NA, azimuth_chirp)


def halves(value):
    high = value.astype(jnp.bfloat16)
    return high, (value - high.astype(jnp.float32)).astype(jnp.bfloat16)


def rounded_halves(value):
    high = lax.reduce_precision(value, 8, 7)
    return high.astype(jnp.bfloat16), (value - high).astype(jnp.bfloat16)


def matrix_left(value):
    high, low = rounded_halves(value)
    return jnp.concatenate([high, high, low], axis=1)


def matrix_right(value):
    high, low = rounded_halves(value)
    return jnp.concatenate([high, high, low], axis=0)


def data_left(value):
    high, low = halves(value)
    return jnp.concatenate([high, low, high], axis=1)


def data_right(value):
    high, low = halves(value)
    return jnp.concatenate([high, low, high], axis=0)


def product(left, right):
    return jnp.dot(left, right, preferred_element_type=jnp.float32)


def dot(left, right):
    return jnp.dot(left, right, precision=HIGHEST, preferred_element_type=jnp.float32)


def roots(count, spread):
    index = np.arange(count)
    return np.exp(-2j * np.pi * ((spread * np.outer(index, index)) % count) / count)


def row_matrix(spread):
    table = roots(PA, spread)
    whole = np.block([[table.real, -table.imag], [table.imag, table.real]]).astype(np.float32)
    return matrix_left(jnp.asarray(whole))


def lane_matrix(table):
    whole = np.block([[table.real, table.imag], [-table.imag, table.real]]).astype(np.float32)
    return jnp.concatenate(rounded_halves(jnp.asarray(whole)), axis=0)


def lane_product(value, lanes_dft):
    high = lanes_dft[: 2 * LANES, :]
    stacked = jnp.concatenate([high, high, lanes_dft[2 * LANES :, :]], axis=0)
    return product(data_left(value), stacked)


def height_lanes():
    return lane_matrix(np.kron(roots(8, 1), np.eye(16)))


def azimuth_lanes():
    return lane_matrix(np.kron(np.eye(8), roots(16, INV)))


def tiles():
    table = np.zeros((LANES, 4, 8, 16), np.float32)
    for o in range(4):
        for k in range(16):
            table[16 * o + k, o, :, k] = 1.0
    return jnp.asarray(table.reshape(LANES, 4 * LANES)).astype(jnp.bfloat16)


def lane_of(shape):
    return lax.broadcasted_iota(jnp.int32, shape, len(shape) - 1)


def row_of(shape):
    return lax.broadcasted_iota(jnp.int32, shape, len(shape) - 2)


def cmul(ar, ai, br, bi):
    return ar * br - ai * bi, ar * bi + ai * br


def dft4(re, im):
    sr, si = re[0] + re[2], im[0] + im[2]
    dr, di = re[0] - re[2], im[0] - im[2]
    tr, ti = re[1] + re[3], im[1] + im[3]
    ur, ui = re[1] - re[3], im[1] - im[3]
    return [sr + tr, dr + ui, sr - tr, dr - ui], [si + ti, di - ur, si - ti, di + ur]


def dft8(re, im):
    half = math.sqrt(0.5)
    er, ei = dft4(re[0::2], im[0::2])
    pr, pi = dft4(re[1::2], im[1::2])
    tr = [pr[0], half * (pr[1] + pi[1]), pi[2], half * (pi[3] - pr[3])]
    ti = [pi[0], half * (pi[1] - pr[1]), -pr[2], -half * (pr[3] + pi[3])]
    out_re = [er[k] + tr[k] for k in range(4)] + [er[k] - tr[k] for k in range(4)]
    out_im = [ei[k] + ti[k] for k in range(4)] + [ei[k] - ti[k] for k in range(4)]
    return out_re, out_im


def dft8_azimuth(re, im):
    out_re, out_im = dft8(re, im)
    order = [(INV * k) % 8 for k in range(8)]
    return [out_re[k] for k in order], [out_im[k] for k in order]


def shift(value, amount):
    amount = amount % LANES
    return value if amount == 0 else pltpu.roll(value, amount, 1)


def trade(parts):
    group = lane_of(parts[0].shape) // 16
    parts = list(parts)
    for bit in (1, 2, 4):
        keep = (group & bit) == 0
        for a in range(8):
            if a & bit == 0:
                low, high = parts[a], parts[a | bit]
                parts[a] = jnp.where(keep, low, shift(high, 16 * bit))
                parts[a | bit] = jnp.where(keep, shift(low, -16 * bit), high)
    return parts


def row_dft(matrix, source, held):
    for i in range(0, 8, 2):
        pair = jnp.concatenate([source(i), source(i + 1)], axis=1)
        result = product(matrix[...], data_right(pair))
        held[i * 128 : (i + 1) * 128, :] = result[:, :LANES]
        held[(i + 1) * 128 : (i + 2) * 128, :] = result[:, LANES:]


def block_of(ref):
    return lambda i: ref[i * 128 : (i + 1) * 128, :]


def re_rows(i, low):
    return slice(i * 128 + low, i * 128 + low + 8)


def im_rows(i, low):
    return slice(i * 128 + 64 + low, i * 128 + 64 + low + 8)


def flat_rows(i, low):
    return slice(i * 64 + low, i * 64 + low + 8)


def pack_kernel(field, out):
    for part in range(field.shape[1] // 64):
        rows = [field.at[0][pl.ds(64 * part + g, 8, stride=8), :] for g in range(8)]
        for e, value in enumerate(trade(rows)):
            out[e, 8 * part : 8 * part + 8, :] = value


def columns_kernel(
    place, got, chirp_re, chirp_im, outer_re, outer_im, inner_re, inner_im, last_re, last_im, split, lanes_dft,
    pick, terrain, out, token, work, held, mid,
):
    e = place[0]
    token[...] = jnp.zeros_like(token)
    for group in range(8):
        low = 8 * group
        re, im = [], []
        for i in range(8):
            at = flat_rows(i, low)
            r, m = cmul(got[re_rows(i, low), :], got[im_rows(i, low), :], chirp_re[at, :], chirp_im[at, :])
            re.append(r)
            im.append(m)
        re, im = dft8(re, im)
        for i in range(8):
            at = flat_rows(i, low)
            r, m = cmul(re[i], im[i], outer_re[at, :], outer_im[at, :])
            work[re_rows(i, low), :] = r
            work[im_rows(i, low), :] = m
    row_dft(split, block_of(work), held)
    ir, ii = inner_re[...], inner_im[...]
    for i in range(8):
        at = slice(i * 64, i * 64 + 64)
        r, m = cmul(held[i * 128 : i * 128 + 64, :], held[i * 128 + 64 : i * 128 + 128, :], ir, ii)
        mid[at, :LANES] = r
        mid[at, LANES:] = m
    result = lane_product(mid[...], lanes_dft)
    r, m = cmul(result[:, :LANES], result[:, LANES:], last_re[...], last_im[...])
    out[pl.ds(0, ROWS, stride=3), :] = r
    out[pl.ds(1, ROWS, stride=3), :] = m
    lane8 = lane_of((8, LANES))
    picks = pltpu.roll(jnp.broadcast_to(pick[...].astype(jnp.float32), (8, LANES)), LANES - 16 * e, 1)
    lows = pltpu.roll(
        jnp.broadcast_to(terrain[...].astype(jnp.float32), (8, LANES)), lax.rem(LANES + 16 - 16 * e, LANES), 1
    )
    aux = jnp.where(lane8 < 16, picks, jnp.where(lane8 < 32, lows, 0.0))
    out[pl.ds(2, ROWS, stride=3), :] = jnp.broadcast_to(aux[None], (PA, 8, LANES)).reshape(ROWS, LANES)


def select_profile(picks, table):
    bits = picks.astype(jnp.int32)
    level = [table[p : p + 1, :] for p in range(16)]
    for bit in (1, 2, 4, 8):
        test = (bits & bit) != 0
        level = [jnp.where(test, level[k + 1], level[k]) for k in range(0, len(level), 2)]
    return level[0]


def rows_kernel(
    place, got, split, tile, outer_re, outer_im, lanes_dft, back_re, back_im, inner_re, inner_im,
    screen_re, screen_im, out, token, work, held, mid, picks, lows, low_strip,
):
    e, f = place[0], place[1]
    token[...] = jnp.zeros_like(token)

    def received(i):
        return jnp.concatenate(
            [got[pl.ds(i * 192, 64, stride=3), :], got[pl.ds(i * 192 + 1, 64, stride=3), :]], axis=0
        )

    row_dft(split, received, held)
    for i in range(8):
        parts = [got[pl.ds(i * 192 + 2 + 3 * o, 16, stride=12), :] for o in range(4)]
        upright = jnp.concatenate(parts + parts, axis=0).T
        spread = product(upright[:32].astype(jnp.bfloat16), tile[...])
        for o in range(4):
            at = (i // 4 + 2 * o) * 64 + 16 * (i % 4)
            picks[at : at + 16, :] = spread[:16, o * LANES : (o + 1) * LANES]
            lows[at : at + 16, :] = spread[16:, o * LANES : (o + 1) * LANES]
    for group in range(8):
        low = 8 * group
        re, im = [], []
        for i in range(8):
            at = flat_rows(i, low)
            r, m = cmul(held[re_rows(i, low), :], held[im_rows(i, low), :], outer_re[at, :], outer_im[at, :])
            re.append(r)
            im.append(m)
        re, im = dft8_azimuth(re, im)
        for i in range(8):
            r, m = cmul(re[i], im[i], inner_re[i : i + 1, :], inner_im[i : i + 1, :])
            mid[flat_rows(i, low), :LANES] = r
            mid[flat_rows(i, low), LANES:] = m
    result = lane_product(mid[...], lanes_dft)
    lane8 = lane_of((8, LANES))
    height = (e + 8 * f + 512 * (lane8 // 16)).astype(jnp.float32)
    for n in range(0, ROWS, 8):
        at = slice(n, n + 8)
        above = height >= lows[at, :]
        sr = jnp.where(above, select_profile(picks[at, :], screen_re), 0.0)
        si = jnp.where(above, select_profile(picks[at, :], screen_im), 0.0)
        br, bi = back_re[at, :], back_im[at, :]
        r, m = cmul(sr, si, br, bi)
        r, m = cmul(result[at, :LANES], result[at, LANES:], r, m)
        low_strip[at, :] = jnp.where(lane8 < 16, r, shift(m, 16))
        r, m = cmul(r, m, br, bi)
        mid[at, :LANES] = r
        mid[at, LANES:] = m
    result = lane_product(mid[...], lanes_dft)
    for group in range(8):
        low = 8 * group
        re, im = [], []
        for i in range(8):
            at = flat_rows(i, low)
            r, m = cmul(result[at, :LANES], result[at, LANES:], inner_re[i : i + 1, :], inner_im[i : i + 1, :])
            re.append(r)
            im.append(m)
        re, im = dft8_azimuth(re, im)
        for i in range(8):
            at = flat_rows(i, low)
            r, m = cmul(re[i], im[i], outer_re[at, :], outer_im[at, :])
            work[re_rows(i, low), :] = r
            work[im_rows(i, low), :] = m
    row_dft(split, block_of(work), held)
    for i in range(8):
        out[pl.ds(i * 192, 64, stride=3), :] = held[i * 128 : i * 128 + 64, :]
        out[pl.ds(i * 192 + 1, 64, stride=3), :] = held[i * 128 + 64 : i * 128 + 128, :]
    lane16 = lane_of((16, LANES))
    for i in range(8):
        block = low_strip[i * 64 : i * 64 + 64, :]
        upright = jnp.concatenate([block, block], axis=0).T
        for part in range(4):
            re = shift(upright[:16], -16 * part)
            im = shift(upright[16:32], 16 - 16 * part)
            to = 4 * (i % 2) + part
            out[pl.ds(to * 192 + 2 + 3 * (i // 2), 16, stride=12), :] = jnp.where(
                lane16 < 16, re, jnp.where(lane16 < 32, im, 0.0)
            )


def final_kernel(
    got, chirp_re, chirp_im, outer_re, outer_im, inner_re, inner_im, coef_re, coef_im, split, lanes_dft,
    seen, range_pair, out, work, held, mid,
):
    for i in range(8):
        at = slice(i * 64, i * 64 + 64)
        r, m = cmul(
            got[pl.ds(i * 192, 64, stride=3), :],
            got[pl.ds(i * 192 + 1, 64, stride=3), :],
            chirp_re[at, :],
            chirp_im[at, :],
        )
        mid[at, :LANES] = r
        mid[at, LANES:] = m
    result = lane_product(mid[...], lanes_dft)
    ir, ii = inner_re[...], inner_im[...]
    for i in range(8):
        at = slice(i * 64, i * 64 + 64)
        r, m = cmul(result[at, :LANES], result[at, LANES:], ir, ii)
        work[i * 128 : i * 128 + 64, :] = r
        work[i * 128 + 64 : i * 128 + 128, :] = m
    row_dft(split, block_of(work), held)
    strip_re, strip_im = [], []
    for group in range(8):
        low = 8 * group
        re, im = [], []
        for i in range(8):
            at = flat_rows(i, low)
            r, m = cmul(held[re_rows(i, low), :], held[im_rows(i, low), :], outer_re[at, :], outer_im[at, :])
            re.append(r)
            im.append(m)
        re, im = dft8(re, im)
        for i in range(8):
            at = flat_rows(i, low)
            r, m = cmul(re[i], im[i], coef_re[at, :], coef_im[at, :])
            out[i * PART + low : i * PART + low + 8, :] = r
            out[i * PART + 64 + low : i * PART + 64 + low + 8, :] = m
            if i == 0 and group < 2:
                strip_re.append(r)
                strip_im.append(m)
    lane16 = lane_of((16, LANES))
    first_re = jnp.zeros((16, LANES), jnp.float32)
    first_im = jnp.zeros((16, LANES), jnp.float32)
    for i in range(8):
        aux = got[pl.ds(i * 192 + 2, 16, stride=3), :]
        here = lane16 // 16 == i
        first_re = jnp.where(here, shift(aux, 16 * i), first_re)
        first_im = jnp.where(here, shift(aux, 16 * i - 16), first_im)
    parts = [(first_re, first_im), (jnp.concatenate(strip_re, axis=0), jnp.concatenate(strip_im, axis=0))]
    power = [seen[...] * (re * re + im * im) for re, im in parts]
    tall = []
    for g in range(8):
        second = jnp.where(lane16 < 32, shift(power[1], 16 - 16 * g), 0.0)
        tall.append(jnp.where(lane16 < 16, shift(power[0], -16 * g), second))
    ranged = product(range_pair[...], data_right(jnp.concatenate(tall, axis=0)))
    for s in range(2):
        spread = jnp.zeros((16, LANES), jnp.float32)
        for g in range(8):
            moved = shift(ranged[16 * g : 16 * g + 16, :], 16 * g - 16 * s)
            spread = jnp.where(lane16 // 16 == g, moved, spread)
        for n, value in enumerate((spread, *parts[s])):
            for i in range(8):
                at = i * PART + 128 + 2 * (3 * s + n)
                out[at : at + 2, :] = value[2 * i : 2 * i + 2, :]
    for i in range(8):
        out[i * PART + 140 : i * PART + 144, :] = jnp.zeros((4, LANES), jnp.float32)


def strips_kernel(got, measured, edges, strips, rows):
    parts = [got[e * PART + 128 : e * PART + 144, :] for e in range(8)]
    for g, value in enumerate(trade(parts)):
        rows[pl.ds(g, 16, stride=8), :] = value
    for s in range(2):
        edges[16 * s : 16 * s + 16, :] = rows[48 * s : 48 * s + 16, :]
        edges[32 + 16 * s : 48 + 16 * s, :] = measured[s]
        strips[32 * s : 32 * s + 32, :] = rows[48 * s + 16 : 48 * s + 48, :]


def unpack_kernel(got, field_out):
    for part in range(got.shape[1] // 8):
        values = trade([got[e, 8 * part : 8 * part + 8, :] for e in range(8)])
        for g, value in enumerate(values):
            field_out.at[0][pl.ds(64 * part + g, 8, stride=8), :] = value


def sources_kernel(place, left, own, right, strips, mask, beams, sources):
    near = jnp.concatenate([left[:32, :], own[:32, :], right[:32, :]], axis=1)
    far = jnp.concatenate([left[32:, :], own[32:, :], right[32:, :]], axis=1)
    back = product(data_left(jnp.concatenate([near, far], axis=1)), beams[...])
    seen = mask[pl.ds(pl.multiple_of(16 * place[0], 16), 16), :].astype(jnp.float32)
    for s in range(2):
        for c in range(2):
            at = 32 * s + 16 * c
            sources[s, c] = 2.0 * seen * strips[at : at + 16, :] * back[16 * s : 16 * s + 16, :]


def screen(height, angle):
    depth = jnp.maximum(height.astype(jnp.float32) - 0.75 * NH, 0.0) / (0.25 * NH)
    amount = abs(GAIN) * jnp.exp(-4.0 * depth * depth)
    turn = angle + float(np.angle(GAIN))
    return amount * jnp.cos(turn), amount * jnp.sin(turn)


def profiles_kernel(place, token, profile, screen_re, screen_im):
    e, f = place[0], place[1]
    lane16 = lane_of((16, LANES))
    group = lane16 // 16
    wide = lane_of((16, 512))
    phase = jnp.zeros((16, LANES), jnp.float32)
    for g in range(8):
        chosen = jnp.where(wide == e + 8 * f, profile[:, 512 * g : 512 * (g + 1)], 0.0)
        phase = jnp.where(group == g, jnp.sum(chosen, axis=1, keepdims=True), phase)
    sr, si = screen(e + 8 * f + 512 * group, phase)
    screen_re[...] = sr
    screen_im[...] = si


def prepare_kernel(
    place, token, profile, pick, terrain, mask, chirp_re, chirp_im, coef_re, coef_im, seen, turned,
):
    e = place[0]
    lane16 = lane_of((16, LANES))
    group = lane16 // 16
    picks = jnp.zeros((8, LANES), jnp.float32)
    lows = jnp.zeros((8, LANES), jnp.float32)
    masks = jnp.zeros((16, LANES), jnp.float32)
    group8 = lane_of((8, LANES)) // 16
    wide_pick = jnp.broadcast_to(pick[...].astype(jnp.float32), (8, LANES))
    wide_low = jnp.broadcast_to(terrain[...].astype(jnp.float32), (8, LANES))
    for g in range(8):
        amount = lax.rem(LANES + 16 * g - 16 * e, LANES)
        picks = jnp.where(group8 == g, pltpu.roll(wide_pick, amount, 1), picks)
        lows = jnp.where(group8 == g, pltpu.roll(wide_low, amount, 1), lows)
        part = mask[pl.ds(g, 16, stride=8), :].astype(jnp.float32)
        masks = jnp.where(group == g, pltpu.roll(part, amount, 1), masks)
    seen[...] = masks
    square_row = row_of((LANES, LANES))
    square_lane = lane_of((LANES, LANES))
    wanted = jnp.broadcast_to(picks[0:1, :], (LANES, LANES))
    match = ((square_row % 16).astype(jnp.float32) == wanted) & (square_row // 16 == square_lane // 16)
    onehot = jnp.where(match, 1.0, 0.0)
    for n in range(NH // LANES):
        block = profile[:, LANES * n : LANES * (n + 1)]
        turned[LANES * n : LANES * (n + 1), :] = jnp.concatenate([block] * 8, axis=0).T
    lanes = lane_of((64, LANES))
    rows = row_of((64, LANES))
    for i in range(8):
        mixed = jnp.zeros((64, LANES), jnp.float32)
        for g in range(8):
            mixed = jnp.where(lanes // 16 == g, turned[pl.ds(512 * i + g, 64, stride=8), :], mixed)
        height = 512 * i + 8 * rows + lanes // 16
        sr, si = screen(height, dot(mixed, onehot))
        above = height.astype(jnp.float32) >= jnp.broadcast_to(lows[0:1, :], (64, LANES))
        at = slice(i * 64, i * 64 + 64)
        r, m = cmul(jnp.where(above, sr, 0.0), jnp.where(above, si, 0.0), chirp_re[at, :], chirp_im[at, :])
        coef_re[at, :] = r
        coef_im[at, :] = m


def turns(steps, modulus):
    angle = (steps % modulus).astype(jnp.float32) * (2.0 * math.pi / modulus)
    return jnp.cos(angle), jnp.sin(angle)


def digits():
    row = lax.broadcasted_iota(jnp.int32, (ROWS, LANES), 0)
    lane = lax.broadcasted_iota(jnp.int32, (ROWS, LANES), 1)
    return row // PA, row % PA, lane // 16, lane % 16


def height_tables(e, f, zero):
    i, j, g, t = digits()
    row = lax.broadcasted_iota(jnp.int32, (PA, LANES), 0)
    group = lax.broadcasted_iota(jnp.int32, (PA, LANES), 1) // 16
    return (
        turns(64 * j * j + g * g + 1024 * i * g + 16 * j * g + zero, 2 * NH),
        turns(zero - i * (8 * j + g), NH),
        turns(zero - row * group, 512),
        turns(
            2 * (i * i + 64 * j * j + 16 * i * j + 1024 * i * g)
            + INV * ((256 * e * e + t * t + 4096 * e * f + 256 * f * t + 32 * e * t) % (2 * NA))
            + zero,
            2 * NA,
        ),
    )


def azimuth_tables(zero):
    i, j, g, t = digits()
    block = lax.broadcasted_iota(jnp.int32, (8, LANES), 0)
    inside = lax.broadcasted_iota(jnp.int32, (8, LANES), 1) % 16
    reverse = (j * j + 4096 * i * i + 128 * i * j + 1024 * j * t) % (2 * NA)
    return (
        turns(zero - (INV % NA) * (j * (16 * i + t)), NA),
        turns(zero - (INV % 128) * block * inside, 128),
        turns(INV * reverse + zero, 2 * NA),
    )


def band(taps, offset):
    hit = offset[..., None] == lax.broadcasted_iota(jnp.int32, (1,) * offset.ndim + (taps.shape[0],), offset.ndim)
    return jnp.sum(jnp.where(hit, taps, 0.0), axis=-1)


def clutter_tables(pulse, beam, measured, eh):
    half = (pulse.shape[0] - 1) // 2
    row = lax.broadcasted_iota(jnp.int32, (BOT, BOT), 0)
    col = lax.broadcasted_iota(jnp.int32, (BOT, BOT), 1)
    adjoint = band(pulse, row - col + half)
    moved = adjoint.reshape(16, 8, BOT).swapaxes(0, 1).reshape(BOT, BOT)
    range_pair = jnp.einsum("ir,hr->ih", moved, moved, precision=HIGHEST)
    own = lax.dynamic_slice_in_dim(adjoint, 16 * eh, 16, 0)
    turned = jnp.einsum("hr,sra->sha", own, measured, precision=HIGHEST)
    taps = beam.shape[0]
    reach = (taps - 1) // 2
    at = lax.broadcasted_iota(jnp.int32, (3 * LANES, LANES), 0) - LANES
    col = lax.broadcasted_iota(jnp.int32, (3 * LANES, LANES), 1)
    first = lax.broadcasted_iota(jnp.int32, (taps, 2 * taps - 1), 0)
    ahead = lax.broadcasted_iota(jnp.int32, (taps, 2 * taps - 1), 1) - (taps - 1)
    auto = jnp.sum(beam[:, None] * band(beam, first + ahead), axis=0)
    pair = band(auto, at - col + taps - 1)
    back = band(beam, col - at + reach)
    return matrix_left(range_pair), turned, matrix_right(jnp.concatenate([pair, -back], axis=0))


VMEM = pl.BlockSpec(memory_space=pltpu.VMEM)
SMEM = pl.BlockSpec(memory_space=pltpu.SMEM)


def f32(*shape):
    return jax.ShapeDtypeStruct(shape, jnp.float32)


def placed(kernel, *refs):
    return kernel((lax.axis_index("ha"), lax.axis_index("az")), *refs)


def call(kernel, outs, scratch, args, place=None, cost=2_000_000, grant=GRANT, interpret=False):
    specs = [VMEM] * len(args)
    if place == "here":
        kernel = functools.partial(placed, kernel)
    elif place is not None:
        specs, args = [SMEM] + specs, (place, *args)
    return pl.pallas_call(
        kernel,
        out_shape=outs,
        in_specs=specs,
        out_specs=jax.tree.map(lambda _: VMEM, outs),
        scratch_shapes=[pltpu.VMEM(shape, jnp.float32) for shape in scratch],
        cost_estimate=pl.CostEstimate(flops=cost * 100, bytes_accessed=cost, transcendentals=0),
        compiler_params=pltpu.CompilerParams(vmem_limit_bytes=grant),
        interpret=interpret,
    )(*args)


WORK = [(2 * ROWS, LANES), (2 * ROWS, LANES), (ROWS, 2 * LANES)]


def gridded(kernel, outs, value, in_block, out_block, in_map, out_map, grant, interpret=False):
    return pl.pallas_call(
        kernel,
        out_shape=outs,
        grid=(2, 2),
        in_specs=[pl.BlockSpec(in_block, in_map)],
        out_specs=pl.BlockSpec(out_block, out_map),
        cost_estimate=pl.CostEstimate(flops=200_000_000, bytes_accessed=2_000_000, transcendentals=0),
        compiler_params=pltpu.CompilerParams(vmem_limit_bytes=grant),
        interpret=interpret,
    )(value)


def stage_pack(field, **kw):
    slab, mixed = (1, 256, LANES), (PH, 32, LANES)
    outs = f32(PH, 2 * PA, LANES)
    moved = gridded(
        pack_kernel, outs, field, slab, mixed, lambda c, p: (c, p, 0), lambda c, p: (0, 2 * c + p, 0), WIDE_GRANT, **kw
    )
    return moved.reshape(2 * ROWS, LANES)


def stage_columns(place, got, heights, pick, terrain, **kw):
    chirp, outer, inner, last = heights
    args = (got, *chirp, *outer, *inner, *last, row_matrix(1), height_lanes(), pick[None], terrain[None])
    return call(columns_kernel, (f32(3 * ROWS, LANES), f32(8, LANES)), WORK, args, place, **kw)


def stage_rows(place, got, azimuths, screen, **kw):
    outer, inner, back = azimuths
    far = (row_matrix(INV), tiles(), *outer, azimuth_lanes(), *back)
    args = (got, *far, *inner, *screen)
    return call(rows_kernel, (f32(3 * ROWS, LANES), f32(8, LANES)), WORK + [(ROWS, LANES)] * 3, args, place, **kw)


def stage_final(got, heights, coef, seen, range_pair, **kw):
    _, outer, inner, chirp = heights
    args = (got, *chirp, *outer, *inner, *coef, row_matrix(1), height_lanes(), seen, range_pair)
    return call(final_kernel, f32(8 * PART, LANES), WORK, args, **kw)


def stage_strips(got, turned, **kw):
    return call(strips_kernel, (f32(64, LANES), f32(64, LANES)), [(BOT, LANES)], (got, turned), **kw)


def stage_unpack(got, **kw):
    slab, mixed = (1, 256, LANES), (PH, 32, LANES)
    outs = f32(2, NH // PH, LANES)
    value = got.reshape(PH, PART, LANES)
    return gridded(
        unpack_kernel, outs, value, mixed, slab, lambda c, p: (0, 2 * c + p, 0), lambda c, p: (c, p, 0), GRANT, **kw
    )


def stage_sources(place, left, own, right, strips, mask, beams, **kw):
    return call(sources_kernel, f32(2, 2, 16, LANES), [], (left, own, right, strips, mask, beams), place, **kw)


def stage_profiles(place, token, profile, **kw):
    return call(profiles_kernel, (f32(16, LANES), f32(16, LANES)), [], (token, profile), place, cost=200_000, **kw)


def stage_prepare(place, token, profile, pick, terrain, mask, heights, **kw):
    outs = (f32(ROWS, LANES), f32(ROWS, LANES), f32(16, LANES))
    args = (token, profile, pick[None], terrain[None], mask, *heights[0])
    return call(prepare_kernel, outs, [(NH, LANES)], args, place, **kw)


def swap_all(rows):
    shaped = rows.reshape(ROWS, 1, 3 * LANES)
    moved = lax.all_to_all(shaped, ("ha", "az"), split_axis=0, concat_axis=0, tiled=True)
    return moved.reshape(rows.shape)


def swap_heights(rows):
    shaped = rows.reshape(PH, rows.shape[0] // PH, LANES)
    return lax.all_to_all(shaped, "ha", split_axis=0, concat_axis=0, tiled=True).reshape(rows.shape)


def local(field, terrain, profile_pick, profile_table, clutter_mask, pulse, beam, measured):
    place = "here"
    range_pair, turned, beams = clutter_tables(pulse, beam, measured, lax.axis_index("ha"))
    e, f = lax.axis_index("ha"), lax.axis_index("az")
    got = swap_heights(stage_pack(field))
    sent, token = stage_columns(place, got, height_tables(e, f, 0), profile_pick, terrain)
    azimuths = azimuth_tables(token[0, 0].astype(jnp.int32))
    screens = stage_profiles(place, token, profile_table)
    got = swap_all(sent)
    sent, token = stage_rows(place, got, azimuths, screens)
    heights = height_tables(e, f, token[0, 0].astype(jnp.int32))
    prepared = stage_prepare(place, token, profile_table, profile_pick, terrain, clutter_mask, heights)
    got = swap_all(sent)
    got = swap_heights(stage_final(got, heights, prepared[0:2], prepared[2], range_pair))
    edges, strips = stage_strips(got, turned)
    left = lax.ppermute(edges, "az", [(i, (i + 1) % PA) for i in range(PA)])
    right = lax.ppermute(edges, "az", [((i + 1) % PA, i) for i in range(PA)])
    field_out = stage_unpack(got)
    return field_out, stage_sources(place, left, edges, right, strips, clutter_mask, beams)


def solution(mesh):
    return jax.shard_map(
        local,
        mesh=mesh,
        in_specs=(
            P(None, "ha", "az"),
            P("az"),
            P("az"),
            P(),
            P(None, "az"),
            P(),
            P(),
            P(None, None, "az"),
        ),
        out_specs=(P(None, "ha", "az"), P(None, None, "ha", "az")),
        check_vma=False,
    )
```

```python
import functools
import math

import jax
import jax.numpy as jnp
import numpy as np
from jax import lax
from jax.experimental import pallas as pl
from jax.experimental.pallas import tpu as pltpu
from jax.sharding import PartitionSpec as P

NH, NA = 4096, 8192
PH, PA = 8, 64
ROWS = PH * PA
LANES = 128
BOT = 128
PART = 144
height_chirp = 1
azimuth_chirp = 3
INV = pow(azimuth_chirp, -1, 2 * NA)
HIGHEST = lax.Precision.HIGHEST
GRANT = 8 * 2**20
WIDE_GRANT = 60 * 2**20


def gauss(count, spread):
    index = np.arange(count, dtype=np.int64)
    return np.sum(np.exp(-1j * np.pi * ((spread * index * index) % (2 * count)) / count)) / count


GAIN = gauss(NH, height_chirp) * gauss(NA, azimuth_chirp)


def halves(value):
    high = value.astype(jnp.bfloat16)
    return high, (value - high.astype(jnp.float32)).astype(jnp.bfloat16)


def rounded_halves(value):
    high = lax.reduce_precision(value, 8, 7)
    return high.astype(jnp.bfloat16), (value - high).astype(jnp.bfloat16)


def matrix_left(value):
    high, low = rounded_halves(value)
    return jnp.concatenate([high, high, low], axis=1)


def matrix_right(value):
    high, low = rounded_halves(value)
    return jnp.concatenate([high, high, low], axis=0)


def data_left(value):
    high, low = halves(value)
    return jnp.concatenate([high, low, high], axis=1)


def data_right(value):
    high, low = halves(value)
    return jnp.concatenate([high, low, high], axis=0)


def product(left, right):
    return jnp.dot(left, right, preferred_element_type=jnp.float32)


def dot(left, right):
    return jnp.dot(left, right, precision=HIGHEST, preferred_element_type=jnp.float32)


def roots(count, spread):
    index = np.arange(count)
    return np.exp(-2j * np.pi * ((spread * np.outer(index, index)) % count) / count)


def row_matrix(spread):
    table = roots(PA, spread)
    whole = np.block([[table.real, -table.imag], [table.imag, table.real]]).astype(np.float32)
    return matrix_left(jnp.asarray(whole))


def lane_matrix(table):
    whole = np.block([[table.real, table.imag], [-table.imag, table.real]]).astype(np.float32)
    return jnp.concatenate(rounded_halves(jnp.asarray(whole)), axis=0)


def lane_product(value, lanes_dft):
    middle = lanes_dft.shape[0] // 2
    high = lanes_dft[:middle, :]
    stacked = jnp.concatenate([high, high, lanes_dft[middle:, :]], axis=0)
    return product(data_left(value), stacked)


def height_lanes():
    return lane_matrix(np.kron(roots(8, 1), np.eye(16)))


def azimuth_lanes():
    return lane_matrix(np.kron(np.eye(8), roots(16, INV)))


def tiles():
    table = np.zeros((LANES, 4, 8, 16), np.float32)
    for o in range(4):
        for k in range(16):
            table[16 * o + k, o, :, k] = 1.0
    return jnp.asarray(table.reshape(LANES, 4 * LANES)).astype(jnp.bfloat16)


def lane_of(shape):
    return lax.broadcasted_iota(jnp.int32, shape, len(shape) - 1)


def row_of(shape):
    return lax.broadcasted_iota(jnp.int32, shape, len(shape) - 2)


def cmul(ar, ai, br, bi):
    return ar * br - ai * bi, ar * bi + ai * br


def dft4(re, im):
    sr, si = re[0] + re[2], im[0] + im[2]
    dr, di = re[0] - re[2], im[0] - im[2]
    tr, ti = re[1] + re[3], im[1] + im[3]
    ur, ui = re[1] - re[3], im[1] - im[3]
    return [sr + tr, dr + ui, sr - tr, dr - ui], [si + ti, di - ur, si - ti, di + ur]


def dft8(re, im):
    half = math.sqrt(0.5)
    er, ei = dft4(re[0::2], im[0::2])
    pr, pi = dft4(re[1::2], im[1::2])
    tr = [pr[0], half * (pr[1] + pi[1]), pi[2], half * (pi[3] - pr[3])]
    ti = [pi[0], half * (pi[1] - pr[1]), -pr[2], -half * (pr[3] + pi[3])]
    out_re = [er[k] + tr[k] for k in range(4)] + [er[k] - tr[k] for k in range(4)]
    out_im = [ei[k] + ti[k] for k in range(4)] + [ei[k] - ti[k] for k in range(4)]
    return out_re, out_im


def dft8_azimuth(re, im):
    out_re, out_im = dft8(re, im)
    order = [(INV * k) % 8 for k in range(8)]
    return [out_re[k] for k in order], [out_im[k] for k in order]


def shift(value, amount):
    amount = amount % LANES
    return value if amount == 0 else pltpu.roll(value, amount, 1)


def trade(parts):
    group = lane_of(parts[0].shape) // 16
    parts = list(parts)
    for bit in (1, 2, 4):
        keep = (group & bit) == 0
        for a in range(8):
            if a & bit == 0:
                low, high = parts[a], parts[a | bit]
                parts[a] = jnp.where(keep, low, shift(high, 16 * bit))
                parts[a | bit] = jnp.where(keep, shift(low, -16 * bit), high)
    return parts


def inner_table():
    steps = (row_of((64, LANES)) * (lane_of((64, LANES)) // 16)) % 512
    angle = steps.astype(jnp.float32) * (2.0 * math.pi / 512)
    return jnp.cos(angle), -jnp.sin(angle)


def row_dft(matrix, source, held):
    for i in range(0, 8, 2):
        pair = jnp.concatenate([source(i), source(i + 1)], axis=1)
        result = product(matrix[...], data_right(pair))
        held[i * 128 : (i + 1) * 128, :] = result[:, :LANES]
        held[(i + 1) * 128 : (i + 2) * 128, :] = result[:, LANES:]


def block_of(ref):
    return lambda i: ref[i * 128 : (i + 1) * 128, :]


def re_rows(i, low):
    return slice(i * 128 + low, i * 128 + low + 8)


def im_rows(i, low):
    return slice(i * 128 + 64 + low, i * 128 + 64 + low + 8)


def flat_rows(i, low):
    return slice(i * 64 + low, i * 64 + low + 8)


def pack_kernel(field, out):
    for part in range(field.shape[1] // 64):
        rows = [field.at[0][pl.ds(64 * part + g, 8, stride=8), :] for g in range(8)]
        for e, value in enumerate(trade(rows)):
            out[e, 8 * part : 8 * part + 8, :] = value


def columns_kernel(
    place, got, chirp_re, chirp_im, outer_re, outer_im, last_re, last_im, split, lanes_dft,
    pick, terrain, seen, turned, out, token, work, held, mid,
):
    e, f = place[0], place[1]
    token[...] = jnp.zeros_like(token)
    for group in range(8):
        low = 8 * group
        re, im = [], []
        for i in range(8):
            at = flat_rows(i, low)
            r, m = cmul(got[re_rows(i, low), :], got[im_rows(i, low), :], chirp_re[at, :], chirp_im[at, :])
            re.append(r)
            im.append(m)
        re, im = dft8(re, im)
        for i in range(8):
            at = flat_rows(i, low)
            r, m = cmul(re[i], im[i], outer_re[at, :], outer_im[at, :])
            work[re_rows(i, low), :] = r
            work[im_rows(i, low), :] = m
    row_dft(split, block_of(work), held)
    ir, ii = inner_table()
    for i in range(8):
        at = slice(i * 64, i * 64 + 64)
        r, m = cmul(held[i * 128 : i * 128 + 64, :], held[i * 128 + 64 : i * 128 + 128, :], ir, ii)
        mid[at, :LANES] = r
        mid[at, LANES:] = m
    result = lane_product(mid[...], lanes_dft)
    r, m = cmul(result[:, :LANES], result[:, LANES:], last_re[...], last_im[...])
    out[pl.ds(0, ROWS, stride=3), :] = r
    out[pl.ds(1, ROWS, stride=3), :] = m
    lane8 = lane_of((8, LANES))
    picks = pltpu.roll(jnp.broadcast_to(pick[...].astype(jnp.float32), (8, LANES)), LANES - 16 * e, 1)
    lows = pltpu.roll(
        jnp.broadcast_to(terrain[...].astype(jnp.float32), (8, LANES)), lax.rem(LANES + 16 - 16 * e, LANES), 1
    )
    common = jnp.where(lane8 < 16, picks, jnp.where(lane8 < 32, lows, 0.0))
    head = jnp.zeros((8, LANES), jnp.float32)
    tail = jnp.zeros((8, LANES), jnp.float32)
    for s in range(2):
        for j in range(2):
            slot = 2 * s + j
            part = turned.at[s][pl.ds(e + 8 * j, 8, stride=16), :]
            here = lane8 // 16 == 4 + slot
            head = jnp.where(here, shift(part, 64 + 16 * slot), head)
            tail = jnp.where(here, shift(part, 80 + 16 * slot), tail)
    lanes = lane_of((64, LANES))
    rows = row_of((64, LANES))
    right = lax.rem(f + 1, PA)
    left = lax.rem(f + PA - 1, PA)
    for i in range(8):
        spread_tail = jnp.broadcast_to(tail[i : i + 1, :], (64, LANES))
        spread_head = jnp.broadcast_to(head[i : i + 1, :], (64, LANES))
        edge = jnp.where(rows == right, spread_tail, jnp.where(rows == left, spread_head, 0.0))
        strip = jnp.concatenate([shift(seen[...], 32 - 16 * i), jnp.zeros((48, LANES), jnp.float32)], axis=0)
        both = jnp.where(lanes < 32, jnp.broadcast_to(common[0:1, :], (64, LANES)), jnp.where(lanes < 48, strip, 0.0))
        out[pl.ds(i * 192 + 2, 64, stride=3), :] = jnp.where(lanes < 64, both, edge)


def select_profile(picks, table):
    bits = picks.astype(jnp.int32)
    level = [table[p : p + 1, :] for p in range(16)]
    for bit in (1, 2, 4, 8):
        test = (bits & bit) != 0
        level = [jnp.where(test, level[k + 1], level[k]) for k in range(0, len(level), 2)]
    return level[0]


def rows_kernel(
    place, got, split, tile, outer_re, outer_im, lanes_dft, back_re, back_im, inner_re, inner_im,
    screen_re, screen_im, out, token, edge, work, held, mid, picks, lows, low_strip,
):
    e, f = place[0], place[1]
    token[...] = jnp.zeros_like(token)

    def received(i):
        return jnp.concatenate(
            [got[pl.ds(i * 192, 64, stride=3), :], got[pl.ds(i * 192 + 1, 64, stride=3), :]], axis=0
        )

    row_dft(split, received, held)
    rows = row_of((64, LANES))
    left = lax.rem(f + PA - 1, PA)
    right = lax.rem(f + 1, PA)
    for i in range(8):
        aux = got[pl.ds(i * 192 + 2, 64, stride=3), :]
        edge[i : i + 1, :] = jnp.sum(jnp.where(rows == left, aux, 0.0), axis=0, keepdims=True)
        edge[8 + i : 9 + i, :] = jnp.sum(jnp.where(rows == right, aux, 0.0), axis=0, keepdims=True)
    for i in range(8):
        parts = [got[pl.ds(i * 192 + 2 + 3 * o, 16, stride=12), :] for o in range(4)]
        upright = jnp.concatenate(parts + parts, axis=0).T
        spread = product(upright[:32].astype(jnp.bfloat16), tile[...])
        for o in range(4):
            at = (i // 4 + 2 * o) * 64 + 16 * (i % 4)
            picks[at : at + 16, :] = spread[:16, o * LANES : (o + 1) * LANES]
            lows[at : at + 16, :] = spread[16:, o * LANES : (o + 1) * LANES]
    for group in range(8):
        low = 8 * group
        re, im = [], []
        for i in range(8):
            at = flat_rows(i, low)
            r, m = cmul(held[re_rows(i, low), :], held[im_rows(i, low), :], outer_re[at, :], outer_im[at, :])
            re.append(r)
            im.append(m)
        re, im = dft8_azimuth(re, im)
        for i in range(8):
            r, m = cmul(re[i], im[i], inner_re[i : i + 1, :], inner_im[i : i + 1, :])
            mid[flat_rows(i, low), :LANES] = r
            mid[flat_rows(i, low), LANES:] = m
    result = lane_product(mid[...], lanes_dft)
    lane8 = lane_of((8, LANES))
    height = (e + 8 * f + 512 * (lane8 // 16)).astype(jnp.float32)
    for n in range(0, ROWS, 8):
        at = slice(n, n + 8)
        above = height >= lows[at, :]
        sr = jnp.where(above, select_profile(picks[at, :], screen_re), 0.0)
        si = jnp.where(above, select_profile(picks[at, :], screen_im), 0.0)
        br, bi = back_re[at, :], back_im[at, :]
        r, m = cmul(sr, si, br, bi)
        r, m = cmul(result[at, :LANES], result[at, LANES:], r, m)
        low_strip[at, :] = jnp.where(lane8 < 16, r, shift(m, 16))
        r, m = cmul(r, m, br, bi)
        mid[at, :LANES] = r
        mid[at, LANES:] = m
    result = lane_product(mid[...], lanes_dft)
    for group in range(8):
        low = 8 * group
        re, im = [], []
        for i in range(8):
            at = flat_rows(i, low)
            r, m = cmul(result[at, :LANES], result[at, LANES:], inner_re[i : i + 1, :], inner_im[i : i + 1, :])
            re.append(r)
            im.append(m)
        re, im = dft8_azimuth(re, im)
        for i in range(8):
            at = flat_rows(i, low)
            r, m = cmul(re[i], im[i], outer_re[at, :], outer_im[at, :])
            work[re_rows(i, low), :] = r
            work[im_rows(i, low), :] = m
    row_dft(split, block_of(work), held)
    lane16 = lane_of((16, LANES))
    lanes = lane_of((64, LANES))
    for i in range(8):
        block = low_strip[i * 64 : i * 64 + 64, :]
        upright = jnp.concatenate([block, block], axis=0).T
        for part in range(4):
            re = shift(upright[:16], -16 * part)
            im = shift(upright[16:32], 16 - 16 * part)
            to = 4 * (i % 2) + part
            picks[pl.ds(to * 64 + i // 2, 16, stride=4), :] = jnp.where(
                lane16 < 16, re, jnp.where(lane16 < 32, im, 0.0)
            )
    for i in range(8):
        at = slice(i * 64, i * 64 + 64)
        known = jnp.where(lanes < 48, got[pl.ds(i * 192 + 2, 64, stride=3), :], 0.0)
        picks[at, :] = jnp.where(lanes < 32, picks[at, :], known)
    for i in range(8):
        source = 6 + i // 2 if i < 4 else (i - 4) // 2
        amount = 1 if i < 4 else PA - 1
        odd = i % 2
        out[pl.ds(i * 256, 64, stride=4), :] = held[i * 128 : i * 128 + 64, :]
        out[pl.ds(i * 256 + 1, 64, stride=4), :] = held[i * 128 + 64 : i * 128 + 128, :]
        re = shift(held[source * 128 : source * 128 + 64, :], -8 * odd)
        im = shift(held[source * 128 + 64 : source * 128 + 128, :], 8 - 8 * odd)
        out[pl.ds(i * 256 + 3, 64, stride=4), :] = pltpu.roll(jnp.where(lanes % 16 < 8, re, im), amount, 0)
        beyond = pltpu.roll(picks[source * 64 : source * 64 + 64, :], amount, 0)
        moved = jnp.where(
            lanes < 56,
            shift(beyond, 48 - 8 * odd),
            jnp.where(lanes < 64, shift(beyond, 40 - 8 * odd), shift(beyond, 32 - 8 * odd)),
        )
        own = picks[i * 64 : i * 64 + 64, :]
        out[pl.ds(i * 256 + 2, 64, stride=4), :] = jnp.where(lanes < 48, own, jnp.where(lanes < 72, moved, 0.0))


def final_kernel(
    got, chirp_re, chirp_im, outer_re, outer_im, coef_re, coef_im, split, lanes_dft, seen, range_pair, out, token, work, held, mid,
):
    token[...] = jnp.zeros_like(token)
    ir, ii = inner_table()
    for i in range(8):
        at = slice(i * 64, i * 64 + 64)
        value = got[pl.ds(i * 256 + 3, 64, stride=4), :]
        r, m = cmul(value, shift(value, -8), chirp_re[at, :], chirp_im[at, :])
        mid[at, :LANES] = r
        mid[at, LANES:] = m
    beyond = lane_product(mid[...], lanes_dft)
    few = jnp.concatenate([split[0:16, :], split[64:80, :]], axis=0)
    halo_re = jnp.zeros((16, LANES), jnp.float32)
    halo_im = jnp.zeros((16, LANES), jnp.float32)
    for i in range(0, 8, 2):
        pair = []
        for k in (i, i + 1):
            at = slice(k * 64, k * 64 + 64)
            pair.append(jnp.concatenate(cmul(beyond[at, :LANES], beyond[at, LANES:], ir, ii), axis=0))
        result = product(few, data_right(jnp.concatenate(pair, axis=1)))
        for k in range(2):
            at = slice((i + k) * 64, (i + k) * 64 + 16)
            part = result[:, k * LANES : (k + 1) * LANES]
            r, m = cmul(part[:16], part[16:], outer_re[at, :], outer_im[at, :])
            halo_re = halo_re + r
            halo_im = halo_im + m
    halo = abs(GAIN) * abs(GAIN) * (halo_re * halo_re + halo_im * halo_im)
    for i in range(8):
        at = slice(i * 64, i * 64 + 64)
        r, m = cmul(
            got[pl.ds(i * 256, 64, stride=4), :],
            got[pl.ds(i * 256 + 1, 64, stride=4), :],
            chirp_re[at, :],
            chirp_im[at, :],
        )
        mid[at, :LANES] = r
        mid[at, LANES:] = m
    result = lane_product(mid[...], lanes_dft)
    for i in range(8):
        at = slice(i * 64, i * 64 + 64)
        r, m = cmul(result[at, :LANES], result[at, LANES:], ir, ii)
        work[i * 128 : i * 128 + 64, :] = r
        work[i * 128 + 64 : i * 128 + 128, :] = m
    row_dft(split, block_of(work), held)
    strip_re, strip_im = [], []
    for group in range(8):
        low = 8 * group
        re, im = [], []
        for i in range(8):
            at = flat_rows(i, low)
            r, m = cmul(held[re_rows(i, low), :], held[im_rows(i, low), :], outer_re[at, :], outer_im[at, :])
            re.append(r)
            im.append(m)
        re, im = dft8(re, im)
        for i in range(8):
            at = flat_rows(i, low)
            r, m = cmul(re[i], im[i], coef_re[at, :], coef_im[at, :])
            out[i * PART + low : i * PART + low + 8, :] = r
            out[i * PART + 64 + low : i * PART + 64 + low + 8, :] = m
            if i == 0 and group < 2:
                strip_re.append(r)
                strip_im.append(m)
    lane16 = lane_of((16, LANES))
    first_re = jnp.zeros((16, LANES), jnp.float32)
    first_im = jnp.zeros((16, LANES), jnp.float32)
    tall_halo = []
    for i in range(8):
        aux = got[pl.ds(i * 256 + 2, 16, stride=4), :]
        square = aux * aux
        first = (shift(square, 32 - 48) + shift(square, 32 - 56)) * shift(aux, 32 - 64)
        second = shift(halo, 40 - 16 * i) * shift(aux, 40 - 64)
        tall_halo.append(jnp.where(lane16 < 40, first, jnp.where(lane16 < 48, second, 0.0)))
        here = lane16 // 16 == i
        first_re = jnp.where(here, shift(aux, 16 * i), first_re)
        first_im = jnp.where(here, shift(aux, 16 * i - 16), first_im)
    parts = [(first_re, first_im), (jnp.concatenate(strip_re, axis=0), jnp.concatenate(strip_im, axis=0))]
    power = [seen[...] * (re * re + im * im) for re, im in parts]
    tall = []
    for g in range(8):
        second = jnp.where(lane16 < 32, shift(power[1], 16 - 16 * g), tall_halo[g])
        tall.append(jnp.where(lane16 < 16, shift(power[0], -16 * g), second))
    ranged = product(range_pair[...], data_right(jnp.concatenate(tall, axis=0)))
    for s in range(2):
        spread = jnp.zeros((16, LANES), jnp.float32)
        for g in range(8):
            moved = shift(ranged[16 * g : 16 * g + 16, :], 16 * g - 16 * s)
            spread = jnp.where(lane16 // 16 == g, moved, spread)
        for n, value in enumerate((spread, *parts[s])):
            for i in range(8):
                at = i * PART + 128 + 2 * (3 * s + n)
                out[at : at + 2, :] = value[2 * i : 2 * i + 2, :]
    spread = jnp.zeros((16, LANES), jnp.float32)
    for g in range(8):
        spread = jnp.where(lane16 // 16 == g, shift(ranged[16 * g : 16 * g + 16, :], 16 * g - 32), spread)
    for i in range(8):
        out[i * PART + 140 : i * PART + 142, :] = spread[2 * i : 2 * i + 2, :]
        out[i * PART + 142 : i * PART + 144, :] = jnp.zeros((2, LANES), jnp.float32)


def unpack_kernel(got, field_out):
    for part in range(got.shape[1] // 8):
        values = trade([got[e, 8 * part : 8 * part + 8, :] for e in range(8)])
        for g, value in enumerate(values):
            field_out.at[0][pl.ds(64 * part + g, 8, stride=8), :] = value


def sources_kernel(place, got, mask, back_measured, beams, sources, rows):
    parts = [got[e * PART + 128 : e * PART + 144, :] for e in range(8)]
    for g, value in enumerate(trade(parts)):
        rows[pl.ds(g, 16, stride=8), :] = value
    seen = mask[pl.ds(pl.multiple_of(16 * place[0], 16), 16), :].astype(jnp.float32)
    for s in range(2):
        ranged = jnp.concatenate([rows[48 * s : 48 * s + 16, :], rows[96:112, :]], axis=1)
        back = product(data_left(ranged), beams[6 * LANES * s : 6 * LANES * (s + 1), :]) - back_measured[s]
        for c in range(2):
            at = 48 * s + 16 + 16 * c
            sources[s, c] = 2.0 * seen * rows[at : at + 16, :] * back


def masks_kernel(place, terrain, mask, seen):
    e = place[0]
    lane16 = lane_of((16, LANES))
    group = lane16 // 16
    low = jnp.broadcast_to(terrain[...].astype(jnp.float32), (16, LANES))
    total = jnp.zeros((16, LANES), jnp.float32)
    for g in range(8):
        amount = lax.rem(LANES + 16 * g - 16 * e, LANES)
        above = (8 * row_of((16, LANES)) + g).astype(jnp.float32) >= low
        part = jnp.where(above, mask[pl.ds(g, 16, stride=8), :].astype(jnp.float32), 0.0)
        total = jnp.where(group == g, pltpu.roll(part, amount, 1), total)
    seen[...] = total


def measured_kernel(place, edge, turned, beam_mix, back_measured):
    e = place[0]
    for s in range(2):
        for j in range(2):
            slot = 2 * s + j
            start = pl.multiple_of(16 * e + 8 * j, 8)
            own = dot(turned.at[s][pl.ds(start, 8), :], beam_mix[LANES : 2 * LANES, :])
            own = own + dot(shift(edge[0:8, :], 64 - 16 * slot), beam_mix[0:LANES, :])
            own = own + dot(shift(edge[8:16, :], 64 - 16 * slot), beam_mix[2 * LANES : 3 * LANES, :])
            back_measured[s, 8 * j : 8 * j + 8, :] = own


def screen(height, angle):
    depth = jnp.maximum(height.astype(jnp.float32) - 0.75 * NH, 0.0) / (0.25 * NH)
    amount = abs(GAIN) * jnp.exp(-4.0 * depth * depth)
    turn = angle + float(np.angle(GAIN))
    return amount * jnp.cos(turn), amount * jnp.sin(turn)


def profiles_kernel(place, token, profile, screen_re, screen_im):
    e, f = place[0], place[1]
    lane16 = lane_of((16, LANES))
    group = lane16 // 16
    wide = lane_of((16, 512))
    phase = jnp.zeros((16, LANES), jnp.float32)
    for g in range(8):
        chosen = jnp.where(wide == e + 8 * f, profile[:, 512 * g : 512 * (g + 1)], 0.0)
        phase = jnp.where(group == g, jnp.sum(chosen, axis=1, keepdims=True), phase)
    sr, si = screen(e + 8 * f + 512 * group, phase)
    screen_re[...] = sr
    screen_im[...] = si


def prepare_kernel(
    place, token, profile, pick, terrain, coef_re, coef_im, turned,
):
    e = place[0]
    picks = jnp.zeros((8, LANES), jnp.float32)
    lows = jnp.zeros((8, LANES), jnp.float32)
    group8 = lane_of((8, LANES)) // 16
    wide_pick = jnp.broadcast_to(pick[...].astype(jnp.float32), (8, LANES))
    wide_low = jnp.broadcast_to(terrain[...].astype(jnp.float32), (8, LANES))
    for g in range(8):
        amount = lax.rem(LANES + 16 * g - 16 * e, LANES)
        picks = jnp.where(group8 == g, pltpu.roll(wide_pick, amount, 1), picks)
        lows = jnp.where(group8 == g, pltpu.roll(wide_low, amount, 1), lows)
    square_row = row_of((LANES, LANES))
    square_lane = lane_of((LANES, LANES))
    wanted = jnp.broadcast_to(picks[0:1, :], (LANES, LANES))
    match = ((square_row % 16).astype(jnp.float32) == wanted) & (square_row // 16 == square_lane // 16)
    onehot = jnp.where(match, 1.0, 0.0)
    for n in range(NH // LANES):
        block = profile[:, LANES * n : LANES * (n + 1)]
        turned[LANES * n : LANES * (n + 1), :] = jnp.concatenate([block] * 8, axis=0).T
    lanes = lane_of((64, LANES))
    rows = row_of((64, LANES))

    @pl.loop(0, 8)
    def block(i):
        mixed = jnp.zeros((64, LANES), jnp.float32)
        for g in range(8):
            mixed = jnp.where(lanes // 16 == g, turned[pl.ds(512 * i + g, 64, stride=8), :], mixed)
        height = 512 * i + 8 * rows + lanes // 16
        g = lanes // 16
        steps = (64 * rows * rows + g * g + 1024 * i * g + 16 * rows * g) % (2 * NH)
        sr, si = screen(height, dot(mixed, onehot) + steps.astype(jnp.float32) * (math.pi / NH))
        above = height.astype(jnp.float32) >= jnp.broadcast_to(lows[0:1, :], (64, LANES))
        at = pl.ds(pl.multiple_of(i * 64, 64), 64)
        coef_re[at, :] = jnp.where(above, sr, 0.0)
        coef_im[at, :] = jnp.where(above, si, 0.0)


def turns(steps, modulus):
    angle = (steps % modulus).astype(jnp.float32) * (2.0 * math.pi / modulus)
    return jnp.cos(angle), jnp.sin(angle)


def digits():
    row = lax.broadcasted_iota(jnp.int32, (ROWS, LANES), 0)
    lane = lax.broadcasted_iota(jnp.int32, (ROWS, LANES), 1)
    return row // PA, row % PA, lane // 16, lane % 16


def height_tables(e, f, zero):
    i, j, g, t = digits()
    return (
        turns(64 * j * j + g * g + 1024 * i * g + 16 * j * g + zero, 2 * NH),
        turns(zero - i * (8 * j + g), NH),
        turns(
            2 * (i * i + 64 * j * j + 16 * i * j + 1024 * i * g)
            + INV * ((256 * e * e + t * t + 4096 * e * f + 256 * f * t + 32 * e * t) % (2 * NA))
            + zero,
            2 * NA,
        ),
    )


def azimuth_tables(zero):
    i, j, g, t = digits()
    block = lax.broadcasted_iota(jnp.int32, (8, LANES), 0)
    inside = lax.broadcasted_iota(jnp.int32, (8, LANES), 1) % 16
    reverse = (j * j + 4096 * i * i + 128 * i * j + 1024 * j * t) % (2 * NA)
    return (
        turns(zero - (INV % NA) * (j * (16 * i + t)), NA),
        turns(zero - (INV % 128) * block * inside, 128),
        turns(INV * reverse + zero, 2 * NA),
    )


def band(taps, offset):
    hit = offset[..., None] == lax.broadcasted_iota(jnp.int32, (1,) * offset.ndim + (taps.shape[0],), offset.ndim)
    return jnp.sum(jnp.where(hit, taps, 0.0), axis=-1)


def clutter_tables(pulse, beam, measured):
    half = (pulse.shape[0] - 1) // 2
    row = lax.broadcasted_iota(jnp.int32, (BOT, BOT), 0)
    col = lax.broadcasted_iota(jnp.int32, (BOT, BOT), 1)
    adjoint = band(pulse, row - col + half)
    moved = adjoint.reshape(16, 8, BOT).swapaxes(0, 1).reshape(BOT, BOT)
    range_pair = jnp.einsum("ir,hr->ih", moved, moved, precision=HIGHEST)
    turned = jnp.einsum("hr,sra->sha", adjoint, measured, precision=HIGHEST)
    taps = beam.shape[0]
    reach = (taps - 1) // 2
    row = lax.broadcasted_iota(jnp.int32, (3 * LANES, LANES), 0)
    col = lax.broadcasted_iota(jnp.int32, (3 * LANES, LANES), 1)
    block, inside = row // LANES, row % LANES
    at = jnp.where(block == 0, inside - 16, jnp.where(block == 1, inside, inside + LANES))
    beam_mix = band(beam, jnp.where((block == 1) | (inside < 16), col - at + reach, -1))
    first = lax.broadcasted_iota(jnp.int32, (taps, 2 * taps - 1), 0)
    ahead = lax.broadcasted_iota(jnp.int32, (taps, 2 * taps - 1), 1) - (taps - 1)
    auto = jnp.sum(beam[:, None] * band(beam, first + ahead), axis=0)
    row = lax.broadcasted_iota(jnp.int32, (2 * LANES, LANES), 0)
    col = lax.broadcasted_iota(jnp.int32, (2 * LANES, LANES), 1)
    inside = row % LANES
    owner, step = inside // 16, (inside // 8) % 2
    halo = jnp.where(owner < 4, 8 * owner - 32, 8 * owner + 96) + inside % 8
    pair = band(auto, jnp.where(row < LANES, row, halo) - col + taps - 1)
    beams = [matrix_right(jnp.where((row < LANES) | (step == s), pair, 0.0)) for s in range(2)]
    return matrix_left(range_pair), turned, beam_mix, jnp.concatenate(beams, axis=0)


VMEM = pl.BlockSpec(memory_space=pltpu.VMEM)
SMEM = pl.BlockSpec(memory_space=pltpu.SMEM)


def f32(*shape):
    return jax.ShapeDtypeStruct(shape, jnp.float32)


def placed(kernel, *refs):
    return kernel((lax.axis_index("ha"), lax.axis_index("az")), *refs)


def call(kernel, outs, scratch, args, place=None, cost=2_000_000, grant=GRANT, interpret=False):
    specs = [VMEM] * len(args)
    if place == "here":
        kernel = functools.partial(placed, kernel)
    elif place is not None:
        specs, args = [SMEM] + specs, (place, *args)
    return pl.pallas_call(
        kernel,
        out_shape=outs,
        in_specs=specs,
        out_specs=jax.tree.map(lambda _: VMEM, outs),
        scratch_shapes=[pltpu.VMEM(shape, jnp.float32) for shape in scratch],
        cost_estimate=pl.CostEstimate(flops=cost * 100, bytes_accessed=cost, transcendentals=0),
        compiler_params=pltpu.CompilerParams(vmem_limit_bytes=grant),
        interpret=interpret,
    )(*args)


WORK = [(2 * ROWS, LANES), (2 * ROWS, LANES), (ROWS, 2 * LANES)]


def gridded(kernel, outs, value, in_block, out_block, in_map, out_map, grant, interpret=False):
    return pl.pallas_call(
        kernel,
        out_shape=outs,
        grid=(2, 2),
        in_specs=[pl.BlockSpec(in_block, in_map)],
        out_specs=pl.BlockSpec(out_block, out_map),
        cost_estimate=pl.CostEstimate(flops=200_000_000, bytes_accessed=2_000_000, transcendentals=0),
        compiler_params=pltpu.CompilerParams(vmem_limit_bytes=grant),
        interpret=interpret,
    )(value)


def stage_pack(field, **kw):
    slab, mixed = (1, 256, LANES), (PH, 32, LANES)
    outs = f32(PH, 2 * PA, LANES)
    moved = gridded(
        pack_kernel, outs, field, slab, mixed, lambda c, p: (c, p, 0), lambda c, p: (0, 2 * c + p, 0), WIDE_GRANT, **kw
    )
    return moved.reshape(2 * ROWS, LANES)


def stage_columns(place, got, heights, pick, terrain, seen, turned, **kw):
    chirp, outer, last = heights
    args = (got, *chirp, *outer, *last, row_matrix(1), height_lanes(), pick[None], terrain[None], seen, turned)
    return call(columns_kernel, (f32(3 * ROWS, LANES), f32(8, LANES)), WORK, args, place, **kw)


def stage_rows(place, got, azimuths, screen, **kw):
    outer, inner, back = azimuths
    far = (row_matrix(INV), tiles(), *outer, azimuth_lanes(), *back)
    args = (got, *far, *inner, *screen)
    return call(rows_kernel, (f32(4 * ROWS, LANES), f32(8, LANES), f32(16, LANES)), WORK + [(ROWS, LANES)] * 3, args, place, **kw)


def stage_final(got, heights, coef, seen, range_pair, **kw):
    _, outer, chirp = heights
    args = (got, *chirp, *outer, *coef, row_matrix(1), height_lanes(), seen, range_pair)
    return call(final_kernel, (f32(8 * PART, LANES), f32(8, LANES)), WORK, args, **kw)


def stage_unpack(got, **kw):
    slab, mixed = (1, 256, LANES), (PH, 32, LANES)
    outs = f32(2, NH // PH, LANES)
    value = got.reshape(PH, PART, LANES)
    return gridded(
        unpack_kernel, outs, value, mixed, slab, lambda c, p: (0, 2 * c + p, 0), lambda c, p: (c, p, 0), GRANT, **kw
    )


def stage_sources(place, got, mask, back_measured, beams, **kw):
    args = (got, mask, back_measured, beams)
    return call(sources_kernel, f32(2, 2, 16, LANES), [(BOT, LANES)], args, place, **kw)


def stage_masks(place, terrain, mask, **kw):
    return call(masks_kernel, f32(16, LANES), [], (terrain[None], mask), place, cost=200_000, **kw)


def stage_measured(place, edge, turned, beam_mix, **kw):
    return call(measured_kernel, f32(2, 16, LANES), [], (edge, turned, beam_mix), place, cost=200_000, **kw)


def stage_profiles(place, token, profile, **kw):
    return call(profiles_kernel, (f32(16, LANES), f32(16, LANES)), [], (token, profile), place, cost=200_000, **kw)


def stage_prepare(place, token, profile, pick, terrain, **kw):
    outs = (f32(ROWS, LANES), f32(ROWS, LANES))
    args = (token, profile, pick[None], terrain[None])
    return call(prepare_kernel, outs, [(NH, LANES)], args, place, **kw)


def swap_all(rows):
    shaped = rows.reshape(ROWS, 1, rows.shape[0] // ROWS * LANES)
    moved = lax.all_to_all(shaped, ("ha", "az"), split_axis=0, concat_axis=0, tiled=True)
    return moved.reshape(rows.shape)


def swap_heights(rows):
    shaped = rows.reshape(PH, rows.shape[0] // PH, LANES)
    return lax.all_to_all(shaped, "ha", split_axis=0, concat_axis=0, tiled=True).reshape(rows.shape)


def local(field, terrain, profile_pick, profile_table, clutter_mask, pulse, beam, measured):
    place = "here"
    range_pair, turned, beam_mix, beams = clutter_tables(pulse, beam, measured)
    e, f = lax.axis_index("ha"), lax.axis_index("az")
    got = swap_heights(stage_pack(field))
    seen = stage_masks(place, terrain, clutter_mask)
    sent, token = stage_columns(place, got, height_tables(e, f, 0), profile_pick, terrain, seen, turned)
    azimuths = azimuth_tables(token[0, 0].astype(jnp.int32))
    screens = stage_profiles(place, token, profile_table)
    got = swap_all(sent)
    sent, token, edge = stage_rows(place, got, azimuths, screens)
    heights = height_tables(e, f, token[0, 0].astype(jnp.int32))
    coef = stage_prepare(place, token, profile_table, profile_pick, terrain)
    back_measured = stage_measured(place, edge, turned, beam_mix)
    got = swap_all(sent)
    sent, _ = stage_final(got, heights, coef, seen, range_pair)
    got = swap_heights(sent)
    return stage_unpack(got), stage_sources(place, got, clutter_mask, back_measured, beams)


def solution(mesh):
    return jax.shard_map(
        local,
        mesh=mesh,
        in_specs=(
            P(None, "ha", "az"),
            P("az"),
            P("az"),
            P(),
            P(None, "az"),
            P(),
            P(),
            P(None, None, "az"),
        ),
        out_specs=(P(None, "ha", "az"), P(None, None, "ha", "az")),
        check_vma=False,
    )
```

```python
import functools
import math

import jax
import jax.numpy as jnp
import numpy as np
from jax import lax
from jax.experimental import pallas as pl
from jax.experimental.pallas import tpu as pltpu
from jax.sharding import PartitionSpec as P

NH, NA = 4096, 8192
PH, PA = 8, 64
ROWS = PH * PA
LANES = 128
BOT = 128
PART = 144
height_chirp = 1
azimuth_chirp = 3
INV = pow(azimuth_chirp, -1, 2 * NA)
HIGHEST = lax.Precision.HIGHEST
GRANT = 8 * 2**20
WIDE_GRANT = 60 * 2**20


def gauss(count, spread):
    index = np.arange(count, dtype=np.int64)
    return np.sum(np.exp(-1j * np.pi * ((spread * index * index) % (2 * count)) / count)) / count


GAIN = gauss(NH, height_chirp) * gauss(NA, azimuth_chirp)


def halves(value):
    high = value.astype(jnp.bfloat16)
    return high, (value - high.astype(jnp.float32)).astype(jnp.bfloat16)


def rounded_halves(value):
    high = lax.reduce_precision(value, 8, 7)
    return high.astype(jnp.bfloat16), (value - high).astype(jnp.bfloat16)


def matrix_left(value):
    high, low = rounded_halves(value)
    return jnp.concatenate([high, high, low], axis=1)


def matrix_right(value):
    high, low = rounded_halves(value)
    return jnp.concatenate([high, high, low], axis=0)


def data_left(value):
    high, low = halves(value)
    return jnp.concatenate([high, low, high], axis=1)


def data_right(value):
    high, low = halves(value)
    return jnp.concatenate([high, low, high], axis=0)


def product(left, right):
    return jnp.dot(left, right, preferred_element_type=jnp.float32)


def dot(left, right):
    return jnp.dot(left, right, precision=HIGHEST, preferred_element_type=jnp.float32)


def roots(count, spread):
    index = np.arange(count)
    return np.exp(-2j * np.pi * ((spread * np.outer(index, index)) % count) / count)


def row_matrix(spread):
    table = roots(PA, spread)
    whole = np.block([[table.real, -table.imag], [table.imag, table.real]]).astype(np.float32)
    return matrix_left(jnp.asarray(whole))


def lane_matrix(table):
    whole = np.block([[table.real, table.imag], [-table.imag, table.real]]).astype(np.float32)
    return jnp.concatenate(rounded_halves(jnp.asarray(whole)), axis=0)


def lane_product(value, lanes_dft):
    middle = lanes_dft.shape[0] // 2
    high = lanes_dft[:middle, :]
    stacked = jnp.concatenate([high, high, lanes_dft[middle:, :]], axis=0)
    return product(data_left(value), stacked)


def height_lanes():
    return lane_matrix(np.kron(roots(8, 1), np.eye(16)))


def azimuth_lanes():
    return lane_matrix(np.kron(np.eye(8), roots(16, INV)))


def tiles():
    table = np.zeros((LANES, 4, 8, 16), np.float32)
    for o in range(4):
        for k in range(16):
            table[16 * o + k, o, :, k] = 1.0
    return jnp.asarray(table.reshape(LANES, 4 * LANES)).astype(jnp.bfloat16)


def lane_of(shape):
    return lax.broadcasted_iota(jnp.int32, shape, len(shape) - 1)


def row_of(shape):
    return lax.broadcasted_iota(jnp.int32, shape, len(shape) - 2)


def cmul(ar, ai, br, bi):
    return ar * br - ai * bi, ar * bi + ai * br


def dft4(re, im):
    sr, si = re[0] + re[2], im[0] + im[2]
    dr, di = re[0] - re[2], im[0] - im[2]
    tr, ti = re[1] + re[3], im[1] + im[3]
    ur, ui = re[1] - re[3], im[1] - im[3]
    return [sr + tr, dr + ui, sr - tr, dr - ui], [si + ti, di - ur, si - ti, di + ur]


def dft8(re, im):
    half = math.sqrt(0.5)
    er, ei = dft4(re[0::2], im[0::2])
    pr, pi = dft4(re[1::2], im[1::2])
    tr = [pr[0], half * (pr[1] + pi[1]), pi[2], half * (pi[3] - pr[3])]
    ti = [pi[0], half * (pi[1] - pr[1]), -pr[2], -half * (pr[3] + pi[3])]
    out_re = [er[k] + tr[k] for k in range(4)] + [er[k] - tr[k] for k in range(4)]
    out_im = [ei[k] + ti[k] for k in range(4)] + [ei[k] - ti[k] for k in range(4)]
    return out_re, out_im


def dft8_azimuth(re, im):
    out_re, out_im = dft8(re, im)
    order = [(INV * k) % 8 for k in range(8)]
    return [out_re[k] for k in order], [out_im[k] for k in order]


def shift(value, amount):
    amount = amount % LANES
    return value if amount == 0 else pltpu.roll(value, amount, 1)


def trade(parts):
    group = lane_of(parts[0].shape) // 16
    parts = list(parts)
    for bit in (1, 2, 4):
        keep = (group & bit) == 0
        for a in range(8):
            if a & bit == 0:
                low, high = parts[a], parts[a | bit]
                parts[a] = jnp.where(keep, low, shift(high, 16 * bit))
                parts[a | bit] = jnp.where(keep, shift(low, -16 * bit), high)
    return parts


def inner_table():
    steps = (row_of((64, LANES)) * (lane_of((64, LANES)) // 16)) % 512
    angle = steps.astype(jnp.float32) * (2.0 * math.pi / 512)
    return jnp.cos(angle), -jnp.sin(angle)


def row_dft(matrix, source, held):
    for i in range(0, 8, 2):
        pair = jnp.concatenate([source(i), source(i + 1)], axis=1)
        result = product(matrix[...], data_right(pair))
        held[i * 128 : (i + 1) * 128, :] = result[:, :LANES]
        held[(i + 1) * 128 : (i + 2) * 128, :] = result[:, LANES:]


def block_of(ref):
    return lambda i: ref[i * 128 : (i + 1) * 128, :]


def re_rows(i, low):
    return slice(i * 128 + low, i * 128 + low + 8)


def im_rows(i, low):
    return slice(i * 128 + 64 + low, i * 128 + 64 + low + 8)


def flat_rows(i, low):
    return slice(i * 64 + low, i * 64 + low + 8)


def pack_kernel(field, out, near, made, came, left):
    gets, puts = [], []
    for n in range(8):
        c, p = divmod(n, 4)
        rows, mixed = pl.ds(128 * p, 128), pl.ds(64 * c + 16 * p, 16)
        gets.append(pltpu.make_async_copy(field.at[c, rows, :], near.at[c, rows, :], came.at[n]))
        puts.append(pltpu.make_async_copy(made.at[:, mixed, :], out.at[:, mixed, :], left.at[n]))
        gets[n].start()
    for n in range(8):
        c, p = divmod(n, 4)
        gets[n].wait()
        for part in (2 * p, 2 * p + 1):
            rows = [near.at[c][pl.ds(64 * part + g, 8, stride=8), :] for g in range(8)]
            for e, value in enumerate(trade(rows)):
                made[e, 64 * c + 8 * part : 64 * c + 8 * part + 8, :] = value
        puts[n].start()
    for put in puts:
        put.wait()


def columns_kernel(
    place, got, chirp_re, chirp_im, outer_re, outer_im, last_re, last_im, split, lanes_dft,
    pick, terrain, seen, turned, out, token, work, held, mid,
):
    e, f = place[0], place[1]
    token[...] = jnp.zeros_like(token)
    for group in range(8):
        low = 8 * group
        re, im = [], []
        for i in range(8):
            at = flat_rows(i, low)
            r, m = cmul(got[re_rows(i, low), :], got[im_rows(i, low), :], chirp_re[at, :], chirp_im[at, :])
            re.append(r)
            im.append(m)
        re, im = dft8(re, im)
        for i in range(8):
            at = flat_rows(i, low)
            r, m = cmul(re[i], im[i], outer_re[at, :], outer_im[at, :])
            work[re_rows(i, low), :] = r
            work[im_rows(i, low), :] = m
    row_dft(split, block_of(work), held)
    ir, ii = inner_table()
    for i in range(8):
        at = slice(i * 64, i * 64 + 64)
        r, m = cmul(held[i * 128 : i * 128 + 64, :], held[i * 128 + 64 : i * 128 + 128, :], ir, ii)
        mid[at, :LANES] = r
        mid[at, LANES:] = m
    result = lane_product(mid[...], lanes_dft)
    r, m = cmul(result[:, :LANES], result[:, LANES:], last_re[...], last_im[...])
    out[pl.ds(0, ROWS, stride=3), :] = r
    out[pl.ds(1, ROWS, stride=3), :] = m
    lane8 = lane_of((8, LANES))
    picks = pltpu.roll(jnp.broadcast_to(pick[...].astype(jnp.float32), (8, LANES)), LANES - 16 * e, 1)
    lows = pltpu.roll(
        jnp.broadcast_to(terrain[...].astype(jnp.float32), (8, LANES)), lax.rem(LANES + 16 - 16 * e, LANES), 1
    )
    common = jnp.where(lane8 < 16, picks, jnp.where(lane8 < 32, lows, 0.0))
    head = jnp.zeros((8, LANES), jnp.float32)
    tail = jnp.zeros((8, LANES), jnp.float32)
    for s in range(2):
        for j in range(2):
            slot = 2 * s + j
            part = turned.at[s][pl.ds(e + 8 * j, 8, stride=16), :]
            here = lane8 // 16 == 4 + slot
            head = jnp.where(here, shift(part, 64 + 16 * slot), head)
            tail = jnp.where(here, shift(part, 80 + 16 * slot), tail)
    lanes = lane_of((64, LANES))
    rows = row_of((64, LANES))
    right = lax.rem(f + 1, PA)
    left = lax.rem(f + PA - 1, PA)
    for i in range(8):
        spread_tail = jnp.broadcast_to(tail[i : i + 1, :], (64, LANES))
        spread_head = jnp.broadcast_to(head[i : i + 1, :], (64, LANES))
        edge = jnp.where(rows == right, spread_tail, jnp.where(rows == left, spread_head, 0.0))
        strip = jnp.concatenate([shift(seen[...], 32 - 16 * i), jnp.zeros((48, LANES), jnp.float32)], axis=0)
        both = jnp.where(lanes < 32, jnp.broadcast_to(common[0:1, :], (64, LANES)), jnp.where(lanes < 48, strip, 0.0))
        out[pl.ds(i * 192 + 2, 64, stride=3), :] = jnp.where(lanes < 64, both, edge)


def select_profile(picks, table):
    bits = picks.astype(jnp.int32)
    level = [table[p : p + 1, :] for p in range(16)]
    for bit in (1, 2, 4, 8):
        test = (bits & bit) != 0
        level = [jnp.where(test, level[k + 1], level[k]) for k in range(0, len(level), 2)]
    return level[0]


def rows_kernel(
    place, got, split, tile, outer_re, outer_im, lanes_dft, back_re, back_im, inner_re, inner_im,
    screen_re, screen_im, out, token, edge, work, held, mid, picks, lows, low_strip,
):
    e, f = place[0], place[1]
    token[...] = jnp.zeros_like(token)

    def received(i):
        return jnp.concatenate(
            [got[pl.ds(i * 192, 64, stride=3), :], got[pl.ds(i * 192 + 1, 64, stride=3), :]], axis=0
        )

    row_dft(split, received, held)
    rows = row_of((64, LANES))
    left = lax.rem(f + PA - 1, PA)
    right = lax.rem(f + 1, PA)
    for i in range(8):
        aux = got[pl.ds(i * 192 + 2, 64, stride=3), :]
        edge[i : i + 1, :] = jnp.sum(jnp.where(rows == left, aux, 0.0), axis=0, keepdims=True)
        edge[8 + i : 9 + i, :] = jnp.sum(jnp.where(rows == right, aux, 0.0), axis=0, keepdims=True)
    for i in range(8):
        parts = [got[pl.ds(i * 192 + 2 + 3 * o, 16, stride=12), :] for o in range(4)]
        upright = jnp.concatenate(parts + parts, axis=0).T
        spread = product(upright[:32].astype(jnp.bfloat16), tile[...])
        for o in range(4):
            at = (i // 4 + 2 * o) * 64 + 16 * (i % 4)
            picks[at : at + 16, :] = spread[:16, o * LANES : (o + 1) * LANES]
            lows[at : at + 16, :] = spread[16:, o * LANES : (o + 1) * LANES]
    for group in range(8):
        low = 8 * group
        re, im = [], []
        for i in range(8):
            at = flat_rows(i, low)
            r, m = cmul(held[re_rows(i, low), :], held[im_rows(i, low), :], outer_re[at, :], outer_im[at, :])
            re.append(r)
            im.append(m)
        re, im = dft8_azimuth(re, im)
        for i in range(8):
            r, m = cmul(re[i], im[i], inner_re[i : i + 1, :], inner_im[i : i + 1, :])
            mid[flat_rows(i, low), :LANES] = r
            mid[flat_rows(i, low), LANES:] = m
    result = lane_product(mid[...], lanes_dft)
    lane8 = lane_of((8, LANES))
    height = (e + 8 * f + 512 * (lane8 // 16)).astype(jnp.float32)
    for n in range(0, ROWS, 8):
        at = slice(n, n + 8)
        above = height >= lows[at, :]
        sr = jnp.where(above, select_profile(picks[at, :], screen_re), 0.0)
        si = jnp.where(above, select_profile(picks[at, :], screen_im), 0.0)
        br, bi = back_re[at, :], back_im[at, :]
        r, m = cmul(sr, si, br, bi)
        r, m = cmul(result[at, :LANES], result[at, LANES:], r, m)
        low_strip[at, :] = jnp.where(lane8 < 16, r, shift(m, 16))
        r, m = cmul(r, m, br, bi)
        mid[at, :LANES] = r
        mid[at, LANES:] = m
    result = lane_product(mid[...], lanes_dft)
    for group in range(8):
        low = 8 * group
        re, im = [], []
        for i in range(8):
            at = flat_rows(i, low)
            r, m = cmul(result[at, :LANES], result[at, LANES:], inner_re[i : i + 1, :], inner_im[i : i + 1, :])
            re.append(r)
            im.append(m)
        re, im = dft8_azimuth(re, im)
        for i in range(8):
            at = flat_rows(i, low)
            r, m = cmul(re[i], im[i], outer_re[at, :], outer_im[at, :])
            work[re_rows(i, low), :] = r
            work[im_rows(i, low), :] = m
    row_dft(split, block_of(work), held)
    lane16 = lane_of((16, LANES))
    lanes = lane_of((64, LANES))
    for i in range(8):
        block = low_strip[i * 64 : i * 64 + 64, :]
        upright = jnp.concatenate([block, block], axis=0).T
        for part in range(4):
            re = shift(upright[:16], -16 * part)
            im = shift(upright[16:32], 16 - 16 * part)
            to = 4 * (i % 2) + part
            picks[pl.ds(to * 64 + i // 2, 16, stride=4), :] = jnp.where(
                lane16 < 16, re, jnp.where(lane16 < 32, im, 0.0)
            )
    for i in range(8):
        at = slice(i * 64, i * 64 + 64)
        known = jnp.where(lanes < 48, got[pl.ds(i * 192 + 2, 64, stride=3), :], 0.0)
        picks[at, :] = jnp.where(lanes < 32, picks[at, :], known)
    for i in range(8):
        source = 6 + i // 2 if i < 4 else (i - 4) // 2
        amount = 1 if i < 4 else PA - 1
        odd = i % 2
        out[pl.ds(i * 256, 64, stride=4), :] = held[i * 128 : i * 128 + 64, :]
        out[pl.ds(i * 256 + 1, 64, stride=4), :] = held[i * 128 + 64 : i * 128 + 128, :]
        re = shift(held[source * 128 : source * 128 + 64, :], -8 * odd)
        im = shift(held[source * 128 + 64 : source * 128 + 128, :], 8 - 8 * odd)
        out[pl.ds(i * 256 + 3, 64, stride=4), :] = pltpu.roll(jnp.where(lanes % 16 < 8, re, im), amount, 0)
        beyond = pltpu.roll(picks[source * 64 : source * 64 + 64, :], amount, 0)
        moved = jnp.where(
            lanes < 56,
            shift(beyond, 48 - 8 * odd),
            jnp.where(lanes < 64, shift(beyond, 40 - 8 * odd), shift(beyond, 32 - 8 * odd)),
        )
        own = picks[i * 64 : i * 64 + 64, :]
        out[pl.ds(i * 256 + 2, 64, stride=4), :] = jnp.where(lanes < 48, own, jnp.where(lanes < 72, moved, 0.0))


def final_kernel(
    got, chirp_re, chirp_im, outer_re, outer_im, coef_re, coef_im, split, lanes_dft, seen, range_pair, out, token, work, held, mid,
):
    token[...] = jnp.zeros_like(token)
    ir, ii = inner_table()
    for i in range(8):
        at = slice(i * 64, i * 64 + 64)
        value = got[pl.ds(i * 256 + 3, 64, stride=4), :]
        r, m = cmul(value, shift(value, -8), chirp_re[at, :], chirp_im[at, :])
        mid[at, :LANES] = r
        mid[at, LANES:] = m
    beyond = lane_product(mid[...], lanes_dft)
    few = jnp.concatenate([split[0:16, :], split[64:80, :]], axis=0)
    halo_re = jnp.zeros((16, LANES), jnp.float32)
    halo_im = jnp.zeros((16, LANES), jnp.float32)
    for i in range(0, 8, 2):
        pair = []
        for k in (i, i + 1):
            at = slice(k * 64, k * 64 + 64)
            pair.append(jnp.concatenate(cmul(beyond[at, :LANES], beyond[at, LANES:], ir, ii), axis=0))
        result = product(few, data_right(jnp.concatenate(pair, axis=1)))
        for k in range(2):
            at = slice((i + k) * 64, (i + k) * 64 + 16)
            part = result[:, k * LANES : (k + 1) * LANES]
            r, m = cmul(part[:16], part[16:], outer_re[at, :], outer_im[at, :])
            halo_re = halo_re + r
            halo_im = halo_im + m
    halo = abs(GAIN) * abs(GAIN) * (halo_re * halo_re + halo_im * halo_im)
    for i in range(8):
        at = slice(i * 64, i * 64 + 64)
        r, m = cmul(
            got[pl.ds(i * 256, 64, stride=4), :],
            got[pl.ds(i * 256 + 1, 64, stride=4), :],
            chirp_re[at, :],
            chirp_im[at, :],
        )
        mid[at, :LANES] = r
        mid[at, LANES:] = m
    result = lane_product(mid[...], lanes_dft)
    for i in range(8):
        at = slice(i * 64, i * 64 + 64)
        r, m = cmul(result[at, :LANES], result[at, LANES:], ir, ii)
        work[i * 128 : i * 128 + 64, :] = r
        work[i * 128 + 64 : i * 128 + 128, :] = m
    row_dft(split, block_of(work), held)
    strip_re, strip_im = [], []
    for group in range(8):
        low = 8 * group
        re, im = [], []
        for i in range(8):
            at = flat_rows(i, low)
            r, m = cmul(held[re_rows(i, low), :], held[im_rows(i, low), :], outer_re[at, :], outer_im[at, :])
            re.append(r)
            im.append(m)
        re, im = dft8(re, im)
        for i in range(8):
            at = flat_rows(i, low)
            r, m = cmul(re[i], im[i], coef_re[at, :], coef_im[at, :])
            out[i * PART + low : i * PART + low + 8, :] = r
            out[i * PART + 64 + low : i * PART + 64 + low + 8, :] = m
            if i == 0 and group < 2:
                strip_re.append(r)
                strip_im.append(m)
    lane16 = lane_of((16, LANES))
    first_re = jnp.zeros((16, LANES), jnp.float32)
    first_im = jnp.zeros((16, LANES), jnp.float32)
    tall_halo = []
    for i in range(8):
        aux = got[pl.ds(i * 256 + 2, 16, stride=4), :]
        square = aux * aux
        first = (shift(square, 32 - 48) + shift(square, 32 - 56)) * shift(aux, 32 - 64)
        second = shift(halo, 40 - 16 * i) * shift(aux, 40 - 64)
        tall_halo.append(jnp.where(lane16 < 40, first, jnp.where(lane16 < 48, second, 0.0)))
        here = lane16 // 16 == i
        first_re = jnp.where(here, shift(aux, 16 * i), first_re)
        first_im = jnp.where(here, shift(aux, 16 * i - 16), first_im)
    parts = [(first_re, first_im), (jnp.concatenate(strip_re, axis=0), jnp.concatenate(strip_im, axis=0))]
    power = [seen[...] * (re * re + im * im) for re, im in parts]
    tall = []
    for g in range(8):
        second = jnp.where(lane16 < 32, shift(power[1], 16 - 16 * g), tall_halo[g])
        tall.append(jnp.where(lane16 < 16, shift(power[0], -16 * g), second))
    ranged = product(range_pair[...], data_right(jnp.concatenate(tall, axis=0)))
    for s in range(2):
        spread = jnp.zeros((16, LANES), jnp.float32)
        for g in range(8):
            moved = shift(ranged[16 * g : 16 * g + 16, :], 16 * g - 16 * s)
            spread = jnp.where(lane16 // 16 == g, moved, spread)
        for n, value in enumerate((spread, *parts[s])):
            for i in range(8):
                at = i * PART + 128 + 2 * (3 * s + n)
                out[at : at + 2, :] = value[2 * i : 2 * i + 2, :]
    spread = jnp.zeros((16, LANES), jnp.float32)
    for g in range(8):
        spread = jnp.where(lane16 // 16 == g, shift(ranged[16 * g : 16 * g + 16, :], 16 * g - 32), spread)
    for i in range(8):
        out[i * PART + 140 : i * PART + 142, :] = spread[2 * i : 2 * i + 2, :]
        out[i * PART + 142 : i * PART + 144, :] = jnp.zeros((2, LANES), jnp.float32)


def finish_kernel(place, got, mask, back_measured, beams, field_out, sources, rows, made, left):
    puts = []
    for n in range(8):
        c, p = divmod(n, 4)
        for part in (2 * p, 2 * p + 1):
            at = 64 * c + 8 * part
            values = trade([got[e * PART + at : e * PART + at + 8, :] for e in range(8)])
            for g, value in enumerate(values):
                made.at[c][pl.ds(64 * part + g, 8, stride=8), :] = value
        piece = pl.ds(128 * p, 128)
        puts.append(pltpu.make_async_copy(made.at[c, piece, :], field_out.at[c, piece, :], left.at[n]))
        puts[n].start()
    parts = [got[e * PART + 128 : e * PART + 144, :] for e in range(8)]
    for g, value in enumerate(trade(parts)):
        rows[pl.ds(g, 16, stride=8), :] = value
    seen = mask[pl.ds(pl.multiple_of(16 * place[0], 16), 16), :].astype(jnp.float32)
    for s in range(2):
        ranged = jnp.concatenate([rows[48 * s : 48 * s + 16, :], rows[96:112, :]], axis=1)
        back = product(data_left(ranged), beams[6 * LANES * s : 6 * LANES * (s + 1), :]) - back_measured[s]
        for c in range(2):
            at = 48 * s + 16 + 16 * c
            sources[s, c] = 2.0 * seen * rows[at : at + 16, :] * back
    for put in puts:
        put.wait()


def masks_kernel(place, terrain, mask, seen):
    e = place[0]
    lane16 = lane_of((16, LANES))
    group = lane16 // 16
    low = jnp.broadcast_to(terrain[...].astype(jnp.float32), (16, LANES))
    total = jnp.zeros((16, LANES), jnp.float32)
    for g in range(8):
        amount = lax.rem(LANES + 16 * g - 16 * e, LANES)
        above = (8 * row_of((16, LANES)) + g).astype(jnp.float32) >= low
        part = jnp.where(above, mask[pl.ds(g, 16, stride=8), :].astype(jnp.float32), 0.0)
        total = jnp.where(group == g, pltpu.roll(part, amount, 1), total)
    seen[...] = total


def measured_kernel(place, edge, turned, beam_mix, back_measured):
    e = place[0]
    for s in range(2):
        for j in range(2):
            slot = 2 * s + j
            start = pl.multiple_of(16 * e + 8 * j, 8)
            own = dot(turned.at[s][pl.ds(start, 8), :], beam_mix[LANES : 2 * LANES, :])
            own = own + dot(shift(edge[0:8, :], 64 - 16 * slot), beam_mix[0:LANES, :])
            own = own + dot(shift(edge[8:16, :], 64 - 16 * slot), beam_mix[2 * LANES : 3 * LANES, :])
            back_measured[s, 8 * j : 8 * j + 8, :] = own


def screen(height, angle):
    depth = jnp.maximum(height.astype(jnp.float32) - 0.75 * NH, 0.0) / (0.25 * NH)
    amount = abs(GAIN) * jnp.exp(-4.0 * depth * depth)
    turn = angle + float(np.angle(GAIN))
    return amount * jnp.cos(turn), amount * jnp.sin(turn)


def profiles_kernel(place, token, profile, screen_re, screen_im):
    e, f = place[0], place[1]
    lane16 = lane_of((16, LANES))
    group = lane16 // 16
    wide = lane_of((16, 512))
    phase = jnp.zeros((16, LANES), jnp.float32)
    for g in range(8):
        chosen = jnp.where(wide == e + 8 * f, profile[:, 512 * g : 512 * (g + 1)], 0.0)
        phase = jnp.where(group == g, jnp.sum(chosen, axis=1, keepdims=True), phase)
    sr, si = screen(e + 8 * f + 512 * group, phase)
    screen_re[...] = sr
    screen_im[...] = si


def prepare_kernel(
    place, token, profile, pick, terrain, coef_re, coef_im, turned,
):
    e = place[0]
    picks = jnp.zeros((8, LANES), jnp.float32)
    lows = jnp.zeros((8, LANES), jnp.float32)
    group8 = lane_of((8, LANES)) // 16
    wide_pick = jnp.broadcast_to(pick[...].astype(jnp.float32), (8, LANES))
    wide_low = jnp.broadcast_to(terrain[...].astype(jnp.float32), (8, LANES))
    for g in range(8):
        amount = lax.rem(LANES + 16 * g - 16 * e, LANES)
        picks = jnp.where(group8 == g, pltpu.roll(wide_pick, amount, 1), picks)
        lows = jnp.where(group8 == g, pltpu.roll(wide_low, amount, 1), lows)
    square_row = row_of((LANES, LANES))
    square_lane = lane_of((LANES, LANES))
    wanted = jnp.broadcast_to(picks[0:1, :], (LANES, LANES))
    match = ((square_row % 16).astype(jnp.float32) == wanted) & (square_row // 16 == square_lane // 16)
    onehot = jnp.where(match, 1.0, 0.0)
    for n in range(NH // LANES):
        block = profile[:, LANES * n : LANES * (n + 1)]
        turned[LANES * n : LANES * (n + 1), :] = jnp.concatenate([block] * 8, axis=0).T
    lanes = lane_of((64, LANES))
    rows = row_of((64, LANES))

    @pl.loop(0, 8)
    def block(i):
        mixed = jnp.zeros((64, LANES), jnp.float32)
        for g in range(8):
            mixed = jnp.where(lanes // 16 == g, turned[pl.ds(512 * i + g, 64, stride=8), :], mixed)
        height = 512 * i + 8 * rows + lanes // 16
        g = lanes // 16
        steps = (64 * rows * rows + g * g + 1024 * i * g + 16 * rows * g) % (2 * NH)
        sr, si = screen(height, dot(mixed, onehot) + steps.astype(jnp.float32) * (math.pi / NH))
        above = height.astype(jnp.float32) >= jnp.broadcast_to(lows[0:1, :], (64, LANES))
        at = pl.ds(pl.multiple_of(i * 64, 64), 64)
        coef_re[at, :] = jnp.where(above, sr, 0.0)
        coef_im[at, :] = jnp.where(above, si, 0.0)


def turns(steps, modulus):
    angle = (steps % modulus).astype(jnp.float32) * (2.0 * math.pi / modulus)
    return jnp.cos(angle), jnp.sin(angle)


def digits():
    row = lax.broadcasted_iota(jnp.int32, (ROWS, LANES), 0)
    lane = lax.broadcasted_iota(jnp.int32, (ROWS, LANES), 1)
    return row // PA, row % PA, lane // 16, lane % 16


def height_tables(e, f, zero):
    i, j, g, t = digits()
    return (
        turns(64 * j * j + g * g + 1024 * i * g + 16 * j * g + zero, 2 * NH),
        turns(zero - i * (8 * j + g), NH),
        turns(
            2 * (i * i + 64 * j * j + 16 * i * j + 1024 * i * g)
            + INV * ((256 * e * e + t * t + 4096 * e * f + 256 * f * t + 32 * e * t) % (2 * NA))
            + zero,
            2 * NA,
        ),
    )


def azimuth_tables(zero):
    i, j, g, t = digits()
    block = lax.broadcasted_iota(jnp.int32, (8, LANES), 0)
    inside = lax.broadcasted_iota(jnp.int32, (8, LANES), 1) % 16
    reverse = (j * j + 4096 * i * i + 128 * i * j + 1024 * j * t) % (2 * NA)
    return (
        turns(zero - (INV % NA) * (j * (16 * i + t)), NA),
        turns(zero - (INV % 128) * block * inside, 128),
        turns(INV * reverse + zero, 2 * NA),
    )


def band(taps, offset):
    hit = offset[..., None] == lax.broadcasted_iota(jnp.int32, (1,) * offset.ndim + (taps.shape[0],), offset.ndim)
    return jnp.sum(jnp.where(hit, taps, 0.0), axis=-1)


def clutter_tables(pulse, beam, measured):
    half = (pulse.shape[0] - 1) // 2
    row = lax.broadcasted_iota(jnp.int32, (BOT, BOT), 0)
    col = lax.broadcasted_iota(jnp.int32, (BOT, BOT), 1)
    adjoint = band(pulse, row - col + half)
    moved = adjoint.reshape(16, 8, BOT).swapaxes(0, 1).reshape(BOT, BOT)
    range_pair = jnp.einsum("ir,hr->ih", moved, moved, precision=HIGHEST)
    turned = jnp.einsum("hr,sra->sha", adjoint, measured, precision=HIGHEST)
    taps = beam.shape[0]
    reach = (taps - 1) // 2
    row = lax.broadcasted_iota(jnp.int32, (3 * LANES, LANES), 0)
    col = lax.broadcasted_iota(jnp.int32, (3 * LANES, LANES), 1)
    block, inside = row // LANES, row % LANES
    at = jnp.where(block == 0, inside - 16, jnp.where(block == 1, inside, inside + LANES))
    beam_mix = band(beam, jnp.where((block == 1) | (inside < 16), col - at + reach, -1))
    first = lax.broadcasted_iota(jnp.int32, (taps, 2 * taps - 1), 0)
    ahead = lax.broadcasted_iota(jnp.int32, (taps, 2 * taps - 1), 1) - (taps - 1)
    auto = jnp.sum(beam[:, None] * band(beam, first + ahead), axis=0)
    row = lax.broadcasted_iota(jnp.int32, (2 * LANES, LANES), 0)
    col = lax.broadcasted_iota(jnp.int32, (2 * LANES, LANES), 1)
    inside = row % LANES
    owner, step = inside // 16, (inside // 8) % 2
    halo = jnp.where(owner < 4, 8 * owner - 32, 8 * owner + 96) + inside % 8
    pair = band(auto, jnp.where(row < LANES, row, halo) - col + taps - 1)
    beams = [matrix_right(jnp.where((row < LANES) | (step == s), pair, 0.0)) for s in range(2)]
    return matrix_left(range_pair), turned, beam_mix, jnp.concatenate(beams, axis=0)


VMEM = pl.BlockSpec(memory_space=pltpu.VMEM)
SMEM = pl.BlockSpec(memory_space=pltpu.SMEM)
FAR = pl.BlockSpec(memory_space=pl.ANY)


def f32(*shape):
    return jax.ShapeDtypeStruct(shape, jnp.float32)


def placed(kernel, *refs):
    return kernel((lax.axis_index("ha"), lax.axis_index("az")), *refs)


def call(kernel, outs, scratch, args, place=None, cost=2_000_000, grant=GRANT, out_specs=None, interpret=False):
    specs = [VMEM] * len(args)
    if place == "here":
        kernel = functools.partial(placed, kernel)
    elif place is not None:
        specs, args = [SMEM] + specs, (place, *args)
    return pl.pallas_call(
        kernel,
        out_shape=outs,
        in_specs=specs,
        out_specs=jax.tree.map(lambda _: VMEM, outs) if out_specs is None else out_specs,
        scratch_shapes=[pltpu.VMEM(s, jnp.float32) if isinstance(s, tuple) else s for s in scratch],
        cost_estimate=pl.CostEstimate(flops=cost * 100, bytes_accessed=cost, transcendentals=0),
        compiler_params=pltpu.CompilerParams(vmem_limit_bytes=grant),
        interpret=interpret,
    )(*args)


WORK = [(2 * ROWS, LANES), (2 * ROWS, LANES), (ROWS, 2 * LANES)]


def stage_pack(field, interpret=False):
    moved = pl.pallas_call(
        pack_kernel,
        out_shape=f32(PH, 2 * PA, LANES),
        in_specs=[FAR],
        out_specs=FAR,
        scratch_shapes=[
            pltpu.VMEM((2, NH // PH, LANES), jnp.float32),
            pltpu.VMEM((PH, 2 * PA, LANES), jnp.float32),
            pltpu.SemaphoreType.DMA((8,)),
            pltpu.SemaphoreType.DMA((8,)),
        ],
        cost_estimate=pl.CostEstimate(flops=200_000_000, bytes_accessed=2_000_000, transcendentals=0),
        compiler_params=pltpu.CompilerParams(vmem_limit_bytes=WIDE_GRANT),
        interpret=interpret,
    )(field)
    return moved.reshape(2 * ROWS, LANES)


def stage_columns(place, got, heights, pick, terrain, seen, turned, **kw):
    chirp, outer, last = heights
    args = (got, *chirp, *outer, *last, row_matrix(1), height_lanes(), pick[None], terrain[None], seen, turned)
    return call(columns_kernel, (f32(3 * ROWS, LANES), f32(8, LANES)), WORK, args, place, **kw)


def stage_rows(place, got, azimuths, screen, **kw):
    outer, inner, back = azimuths
    far = (row_matrix(INV), tiles(), *outer, azimuth_lanes(), *back)
    args = (got, *far, *inner, *screen)
    return call(rows_kernel, (f32(4 * ROWS, LANES), f32(8, LANES), f32(16, LANES)), WORK + [(ROWS, LANES)] * 3, args, place, **kw)


def stage_final(got, heights, coef, seen, range_pair, **kw):
    _, outer, chirp = heights
    args = (got, *chirp, *outer, *coef, row_matrix(1), height_lanes(), seen, range_pair)
    return call(final_kernel, (f32(8 * PART, LANES), f32(8, LANES)), WORK, args, **kw)


def stage_finish(place, got, mask, back_measured, beams, **kw):
    args = (got, mask, back_measured, beams)
    outs = (f32(2, NH // PH, LANES), f32(2, 2, 16, LANES))
    scratch = [(BOT, LANES), (2, NH // PH, LANES), pltpu.SemaphoreType.DMA((8,))]
    return call(finish_kernel, outs, scratch, args, place, out_specs=(FAR, VMEM), **kw)


def stage_masks(place, terrain, mask, **kw):
    return call(masks_kernel, f32(16, LANES), [], (terrain[None], mask), place, cost=200_000, **kw)


def stage_measured(place, edge, turned, beam_mix, **kw):
    return call(measured_kernel, f32(2, 16, LANES), [], (edge, turned, beam_mix), place, cost=200_000, **kw)


def stage_profiles(place, token, profile, **kw):
    return call(profiles_kernel, (f32(16, LANES), f32(16, LANES)), [], (token, profile), place, cost=200_000, **kw)


def stage_prepare(place, token, profile, pick, terrain, **kw):
    outs = (f32(ROWS, LANES), f32(ROWS, LANES))
    args = (token, profile, pick[None], terrain[None])
    return call(prepare_kernel, outs, [(NH, LANES)], args, place, **kw)


def swap_all(rows):
    shaped = rows.reshape(ROWS, 1, rows.shape[0] // ROWS * LANES)
    moved = lax.all_to_all(shaped, ("ha", "az"), split_axis=0, concat_axis=0, tiled=True)
    return moved.reshape(rows.shape)


def swap_heights(rows):
    shaped = rows.reshape(PH, rows.shape[0] // PH, LANES)
    return lax.all_to_all(shaped, "ha", split_axis=0, concat_axis=0, tiled=True).reshape(rows.shape)


def local(field, terrain, profile_pick, profile_table, clutter_mask, pulse, beam, measured):
    place = "here"
    range_pair, turned, beam_mix, beams = clutter_tables(pulse, beam, measured)
    e, f = lax.axis_index("ha"), lax.axis_index("az")
    got = swap_heights(stage_pack(field))
    seen = stage_masks(place, terrain, clutter_mask)
    sent, token = stage_columns(place, got, height_tables(e, f, 0), profile_pick, terrain, seen, turned)
    azimuths = azimuth_tables(token[0, 0].astype(jnp.int32))
    screens = stage_profiles(place, token, profile_table)
    got = swap_all(sent)
    sent, token, edge = stage_rows(place, got, azimuths, screens)
    heights = height_tables(e, f, token[0, 0].astype(jnp.int32))
    coef = stage_prepare(place, token, profile_table, profile_pick, terrain)
    back_measured = stage_measured(place, edge, turned, beam_mix)
    got = swap_all(sent)
    sent, _ = stage_final(got, heights, coef, seen, range_pair)
    got = swap_heights(sent)
    return stage_finish(place, got, clutter_mask, back_measured, beams)


def solution(mesh):
    return jax.shard_map(
        local,
        mesh=mesh,
        in_specs=(
            P(None, "ha", "az"),
            P("az"),
            P("az"),
            P(),
            P(None, "az"),
            P(),
            P(),
            P(None, None, "az"),
        ),
        out_specs=(P(None, "ha", "az"), P(None, None, "ha", "az")),
        check_vma=False,
    )
```
